512 devices in a mesh: space: 16 (over z, x_hi), ens: 32 (over x_lo, y, core).
Axes of the slice: x: 4 (x_hi: 2, x_lo: 2; x = x_hi * 2 + x_lo), y: 8, z: 8, core: 2. Of those that a mesh axis runs over, the one named last changes fastest.
Arguments:
- starting_speed_field: float32 [256, 256, 2048], P('ens', 'space'), may hold values from -6 to 6
- sample_fluidity_exponent: float32 [256, 256, 2048], P('ens', 'space'), may hold values from -1.5 to 0.5
- observed: float32 [4096], P('space'), may hold values from -6 to 6
- obs_noise: float32 [256, 4096], P('ens', 'space'), may hold values from -3 to 3
- obs_var: float32 [4096], P('space'), may hold values from 0.5 to 4
- probe_cells: int32 [4096], P('space'), may hold values from 0 to 32767
- pair_cells: int32 [16, 32], P('space'), may hold values from 0 to 255
- pair_probes: int32 [16, 32], P('space'), may hold values from 0 to 5, as said below
- pair_taper: int32 [16, 32], P('space'), may hold values from 1 to 256
- pair_counts: int32 [16], P('space'), may hold values from 8 to 32, as said below
- probe_taper: int32 [16, 2, 6], P('space'), may hold values from 1 to 256
Outputs:
- prior_speed_prediction: float32 [256, 256, 2048], P('ens', 'space')
- posterior_fluidity_exponent: float32 [256, 256, 2048], P('ens', 'space')
- weighted_innovation_matrix: float32 [256, 4096], P('ens', 'space')
The draws below stay inside these ranges and needn't reach their ends.
Inputs may be any that keep to these rules, and one draw needn't show every extreme that they name: `pair_probes`: each pair slot names a probe block of the slab or of a neighbour slab, never one outside the channel: slab 0 uses 2 to 5 and the last slab 0 to 3. `pair_counts`: slots at or beyond a slab's count are padding; some slab has all 32 slots live.
All inputs are finite; a program needn't handle non-finite values.
Results may differ from the reference program's by a relative error of at most 0.000096.
Values sent between devices are 32-bit elements; how exact they have to be, the bound alone decides.
A program may use at most 64 MiB of HBM per device.

```python
import math
import jax
import jax.numpy as jnp
from jax import lax

BLK = 128
SX = 16
NY = 32
NZ = 64
PBD = 2
PAIR_MAX = 32
STEPS = 2
LAYER_NUMBER = 16
SAMPLE_NUMBER = 256
NX = 256
PLANE = 2048
GRID_POINTS_PER = 32768
CB = 256
PROBE_DEV = 256
NPROBE = 4096


def draw_pair_probes(key, part):
    slab_rows = jnp.arange(LAYER_NUMBER, dtype=jnp.int32)[:, None]
    slot_cols = jnp.arange(PAIR_MAX, dtype=jnp.int32)[None, :]
    low_block = jnp.where(slab_rows == 0, PBD, 0)
    high_block = jnp.where(slab_rows == LAYER_NUMBER - 1, 2 * PBD, 3 * PBD)
    random_bits = jax.random.randint(key, (LAYER_NUMBER, PAIR_MAX), 0, 1 << 20)
    general = low_block + random_bits % (high_block - low_block)
    inside = random_bits % PBD
    lower_side = jnp.where(slab_rows == 0, 2 * PBD + inside, inside)
    upper_side = jnp.where(slab_rows == LAYER_NUMBER - 1, inside, 2 * PBD + inside)
    chosen = jnp.where(slot_cols == 0, lower_side, jnp.where(slot_cols == 1, upper_side, general))
    return chosen.astype(jnp.int32)


def draw_pair_counts(key, part):
    least = max(2, PAIR_MAX // 4)
    counts = jax.random.randint(key, (LAYER_NUMBER,), least, PAIR_MAX + 1)
    fullest = jax.random.randint(jax.random.fold_in(key, 11), (), 0, LAYER_NUMBER)
    return jnp.where(jnp.arange(LAYER_NUMBER, dtype=jnp.int32) == fullest, PAIR_MAX, counts).astype(jnp.int32)


def set_ends(values, rng, low, largest):
    longest = values.shape.index(max(values.shape))
    spots = []
    for shift in (0, 1):
        where = [jax.random.randint(jax.random.fold_in(rng, axis), (), 0, length) for axis, length in enumerate(values.shape)]
        where[longest] = (where[longest] + shift) % values.shape[longest]
        spots.append(tuple(where))
    return values.at[spots[0]].set(low).at[spots[1]].set(largest)


def block_scale(stream_key, extent, pieces, low, high):
    factor_of = 1.0
    for axis_at, shards_of in pieces:
        draws = jax.random.uniform(jax.random.fold_in(jax.random.fold_in(stream_key, 6), axis_at), (shards_of,), jnp.float32, low / len(pieces), high / len(pieces))
        factor_of = factor_of * jnp.repeat(jnp.exp(draws), extent[axis_at] // shards_of).reshape((-1,) + (1,) * (len(extent) - 1 - axis_at))
    return factor_of


def gaussian(stream_key, extent, scale, most, cuts=(), held_as=jnp.bfloat16):
    level = block_scale(stream_key, extent, cuts, -0.22, 0.18) if cuts else 1.0
    result = jax.random.normal(stream_key, extent, jnp.float32) * scale * level
    return jnp.minimum(jnp.maximum(result, -most), most).astype(held_as)


def setup_inputs(seed: int = 0) -> dict:
    arg_keys = jax.random.split(jax.random.key(seed), 12)
    starting_speed_field = gaussian(arg_keys[0], (SAMPLE_NUMBER, NX, PLANE), 1.0, 6.0, ((0, 32), (1, 16)), jnp.float32)
    sample_fluidity_exponent = jnp.clip(-1.5 + 2.0 * jax.random.uniform(arg_keys[1], (SAMPLE_NUMBER, NX, PLANE), jnp.float32) ** block_scale(arg_keys[1], (SAMPLE_NUMBER, NX, PLANE), ((0, 32), (1, 16)), -0.2, 0.2), -1.5, 0.5)
    observed = gaussian(arg_keys[2], (NPROBE,), 1.0, 6.0, ((0, 16),), jnp.float32)
    obs_noise = gaussian(arg_keys[3], (SAMPLE_NUMBER, NPROBE), 0.5, 3.0, ((0, 32), (1, 16)), jnp.float32)
    obs_var = jnp.clip(jnp.exp(math.log(4.0) - 2.0794415 * jax.random.uniform(arg_keys[4], (NPROBE,), jnp.float32) ** block_scale(arg_keys[4], (NPROBE,), ((0, 16),), -0.2, 0.2)), 0.5, 4.0)
    probe_cells = set_ends(jax.random.randint(arg_keys[5], (NPROBE,), 0, SX * NY * NZ), jax.random.fold_in(arg_keys[5], 1), 0, (SX * NY * NZ) - 1).astype(jnp.int32)
    pair_cells = set_ends(jax.random.randint(arg_keys[6], (LAYER_NUMBER, PAIR_MAX), 0, SX * NY * NZ // BLK), jax.random.fold_in(arg_keys[6], 1), 0, (SX * NY * NZ // BLK) - 1).astype(jnp.int32)
    pair_probes = draw_pair_probes(jax.random.fold_in(arg_keys[11], 71), 0)
    pair_taper = set_ends(jax.random.randint(arg_keys[8], (LAYER_NUMBER, PAIR_MAX), 1, 257), jax.random.fold_in(arg_keys[8], 1), 1, 256).astype(jnp.int32)
    pair_counts = draw_pair_counts(jax.random.fold_in(arg_keys[11], 71), 0)
    probe_taper = set_ends(jax.random.randint(arg_keys[10], (LAYER_NUMBER, PBD, 3 * PBD), 1, 257), jax.random.fold_in(arg_keys[10], 1), 1, 256).astype(jnp.int32)
    return dict(starting_speed_field=starting_speed_field, sample_fluidity_exponent=sample_fluidity_exponent, observed=observed, obs_noise=obs_noise, obs_var=obs_var, probe_cells=probe_cells, pair_cells=pair_cells, pair_probes=pair_probes, pair_taper=pair_taper, pair_counts=pair_counts, probe_taper=probe_taper)


DT_STEP = 0.08


def advance(padded_u, padded_t):
    inner_u = padded_u[:, 1:-1]
    inner_t = padded_t[:, 1:-1]
    viscous = jnp.exp(inner_t)
    viscosity_halo_padding = jnp.exp(padded_t)
    running = 0.5 * (viscous + viscosity_halo_padding[:, 2:]) * (padded_u[:, 2:] - inner_u)
    running = running + 0.5 * (viscous + viscosity_halo_padding[:, :-2]) * (padded_u[:, :-2] - inner_u)
    for offset in (NZ, -NZ):
        running = running + 0.5 * (viscous + jnp.roll(viscous, offset, axis=2)) * (jnp.roll(inner_u, offset, axis=2) - inner_u)
    height = lax.broadcasted_iota(jnp.int32, inner_u.shape, 2) % NZ
    for offset, wall_cell in ((1, 0), (-1, NZ - 1)):
        at_wall = height == wall_cell
        beside_u = jnp.where(at_wall, 0.0, jnp.roll(inner_u, offset, axis=2))
        beside_v = jnp.where(at_wall, 1.0, jnp.roll(viscous, offset, axis=2))
        running = running + 0.5 * (viscous + beside_v) * (beside_u - inner_u)
    return inner_u + DT_STEP * running


def reference(starting_speed_field, sample_fluidity_exponent, observed, obs_noise, obs_var, probe_cells, pair_cells, pair_probes, pair_taper, pair_counts, probe_taper):
    highest = lax.Precision.HIGHEST

    def sample_number_current(pair_in):
        current, visc_field = pair_in
        for repeat in range(STEPS):
            padded_u = jnp.pad(current, ((1, 1), (0, 0)))
            padded_t = jnp.pad(visc_field, ((1, 1), (0, 0)))
            current = advance(padded_u[None], padded_t[None])[0]
        return current

    prior_speed_prediction = lax.map(sample_number_current, (starting_speed_field, sample_fluidity_exponent))
    raveled_speed_field = prior_speed_prediction.reshape(SAMPLE_NUMBER, LAYER_NUMBER * GRID_POINTS_PER)
    global_cell = (jnp.arange(NPROBE, dtype=jnp.int32) // PROBE_DEV) * GRID_POINTS_PER + probe_cells
    predicted = raveled_speed_field[:, global_cell]
    anomaly = predicted - jnp.sum(predicted, axis=0) / SAMPLE_NUMBER
    scaled = (observed + obs_noise - predicted) / obs_var

    def extend(values):
        padded = jnp.pad(values, ((0, 0), (PROBE_DEV, PROBE_DEV)))
        window = jnp.arange(LAYER_NUMBER, dtype=jnp.int32)[:, None] * PROBE_DEV + jnp.arange(3 * PROBE_DEV, dtype=jnp.int32)[None, :]
        return padded[:, window].reshape(SAMPLE_NUMBER, LAYER_NUMBER, 3 * PBD, BLK)

    anom_wide = extend(anomaly)
    scaled_wide = extend(scaled)
    own_blocks = anom_wide[:, :, PBD:2 * PBD]
    probe_cov = jnp.einsum('msip,msjq->sijpq', own_blocks, anom_wide, precision=highest)
    probe_cov = probe_cov * (probe_taper.astype(jnp.float32) / 256.0 / (SAMPLE_NUMBER - 1))[:, :, :, None, None]
    correction = jnp.einsum('sijpq,msjq->msip', probe_cov, scaled_wide, precision=highest)
    var_blocks = obs_var.reshape(LAYER_NUMBER, PBD, BLK)
    gain_blocks = scaled_wide[:, :, PBD:2 * PBD] - correction / var_blocks[None]
    weighted_innovation_matrix = gain_blocks.reshape(SAMPLE_NUMBER, NPROBE)
    gain_wide = extend(weighted_innovation_matrix)
    slab_rows = jnp.arange(LAYER_NUMBER, dtype=jnp.int32)[:, None]
    theta_blocks = sample_fluidity_exponent.reshape(SAMPLE_NUMBER, LAYER_NUMBER, CB, BLK)
    theta_pick = theta_blocks[:, slab_rows, pair_cells]
    anom_pick = anom_wide[:, slab_rows, pair_probes]
    gain_pick = gain_wide[:, slab_rows, pair_probes]
    cross_cov = jnp.einsum('mskr,mskq->skrq', theta_pick, anom_pick, precision=highest)
    active_pairs = jnp.arange(PAIR_MAX, dtype=jnp.int32)[None, :] < pair_counts[:, None]
    weight = jnp.where(active_pairs, pair_taper.astype(jnp.float32) / 256.0, 0.0) / (SAMPLE_NUMBER - 1)
    updates = jnp.einsum('skrq,mskq->mskr', cross_cov, gain_pick, precision=highest) * weight[None, :, :, None]
    one_hot = (pair_cells[:, :, None] == jnp.arange(CB, dtype=jnp.int32)[None, None, :]).astype(jnp.float32)
    increment = jnp.einsum('skc,mskr->mscr', one_hot, updates, precision=highest)
    posterior_fluidity_exponent = sample_fluidity_exponent + increment.reshape(sample_fluidity_exponent.shape)
    return prior_speed_prediction, posterior_fluidity_exponent, weighted_innovation_matrix
```

```python
import functools

import jax
import jax.numpy as jnp
from jax import lax
from jax.experimental import pallas as pl
from jax.experimental.pallas import tpu as pltpu
from jax.sharding import PartitionSpec as P

BLK = 128
NZ = 64
DT_STEP = 0.08
COEF = 0.5 * DT_STEP

NS = 16
NYR = 8
G = 4
PLANES = 16
LT = 16
MEM = 8
ALL = 256
SLOTS = 32
SPG = SLOTS // G

MESH = pl.DeviceIdType.MESH
HIGHEST = lax.Precision.HIGHEST
F32 = jnp.float32


def dot(a, b, dims):
    return lax.dot_general(a, b, (dims, ((), ())), precision=HIGHEST, preferred_element_type=F32)


NN = ((1,), (0,))
NT = ((1,), (1,))


def tile(t):
    return slice(t * BLK, (t + 1) * BLK)


def tiles(ref, *where):
    return [ref[(*where, slice(None), tile(t))] for t in range(LT)]


def put(ref, values, *where):
    for t in range(LT):
        ref[(*where, slice(None), tile(t))] = values[t]


def main_kernel(
    u_hbm, t_hbm, obs_hbm, noise_hbm, var_hbm, cells, pair_cells, pair_probes, probe_taper, *refs
):
    (
    prior_hbm, gain_out, upd_out,
    ust, tst, u0, th, vv, cx, cy, cz, cd, uh, thh, ps, pr, u1, u2, ost,
    thg, agb, anom, a_own, a_win, k_own, k_win, us, upd,
    in_sem, out_sem, halo_s, halo_r, sub_s, sub_r, ring_s, ring_r, ag1_s, ag1_r, ag2_s, ag2_r, ax_s, ax_r,
    kx_s, kx_r, ux_s, ux_r,
    obs_ref, noise_ref, var_ref, small_sem,
    ) = refs
    s = lax.axis_index("space")
    e = lax.axis_index("ens")
    xl, y, c = e // (2 * NYR), (e // 2) % NYR, e % 2
    g = xl * 2 + c
    has_up, has_dn = s < NS - 1, s > 0
    s_up, s_dn = jnp.minimum(s + 1, NS - 1), jnp.maximum(s - 1, 0)

    def ens_of(gg, yy):
        return (gg // 2) * (2 * NYR) + yy * 2 + gg % 2

    def remote(src, dst, ss, rs, space, ens):
        return pltpu.make_async_remote_copy(
            src_ref=src, dst_ref=dst, send_sem=ss, recv_sem=rs, device_id=(space, ens), device_id_type=MESH
        )

    sub_g = [(g + d) % G for d in range(1, G)]

    loads = []
    for t in range(LT):
        for k, (src, dst) in enumerate(((t_hbm, tst), (u_hbm, ust))):
            loads.append(pltpu.make_async_copy(src.at[:, tile(t)], dst.at[t], in_sem.at[k * LT + t]))
    for copy in loads:
        copy.start()
    small_src = (obs_hbm, noise_hbm, var_hbm)
    small_dst = (obs_ref, noise_ref, var_ref)
    smalls = [pltpu.make_async_copy(a, b, small_sem.at[i]) for i, (a, b) in enumerate(zip(small_src, small_dst))]
    for copy in smalls:
        copy.start()

    bar = pltpu.get_barrier_semaphore()
    for d in range(1, NYR):
        pl.semaphore_signal(bar, 1, device_id=(s, ens_of(g, (y + d) % NYR)), device_id_type=MESH)
    for gg in sub_g:
        pl.semaphore_signal(bar, 1, device_id=(s, ens_of(gg, y)), device_id_type=MESH)

    @pl.when(has_up)
    def _():
        for gg in range(G):
            pl.semaphore_signal(bar, 1, device_id=(s_up, ens_of(gg, y)), device_id_type=MESH)

    @pl.when(has_dn)
    def _():
        for gg in range(G):
            pl.semaphore_signal(bar, 1, device_id=(s_dn, ens_of(gg, y)), device_id_type=MESH)

    lane = lax.broadcasted_iota(jnp.int32, (MEM, BLK), 1)
    low = lane < NZ
    height = lane % NZ
    top = height == NZ - 1
    wall = (height == 0) | top

    def y_up(x):
        r = [pltpu.roll(v, NZ, 1) for v in x]
        return [jnp.where(low, r[t], r[(t + 1) % LT]) for t in range(LT)]

    def y_down(x):
        r = [pltpu.roll(v, NZ, 1) for v in x]
        return [jnp.where(low, r[t - 1], r[t]) for t in range(LT)]

    def bring(p):
        for t in range(LT):
            rows = pl.ds(p, MEM, PLANES)
            th[p * LT + t] = tst[t, rows, :]
            u0[p, :, tile(t)] = ust[t, rows, :]

    def viscosity(p):
        for t in range(LT):
            vv[p, :, tile(t)] = jnp.exp(th[p * LT + t])

    def loop(lo, hi, fn):
        def body(p, carry):
            fn(p)
            return carry

        lax.fori_loop(lo, hi, body, 0)

    def coefficients(p):
        v = tiles(vv, p)
        vy = y_up(v)
        for t in range(LT):
            cy[p, :, tile(t)] = COEF * (v[t] + vy[t])
            cz[p, :, tile(t)] = jnp.where(top, 0.0, COEF * (v[t] + pltpu.roll(v[t], BLK - 1, 1)))
            cd[p, :, tile(t)] = 1.0 - jnp.where(wall, COEF * (v[t] + 1.0), 0.0)

    def face(p):
        for t in range(LT):
            cx[p, :, tile(t)] = COEF * (vv[p - 1, :, tile(t)] + vv[p, :, tile(t)])

    def partial(src, off, p, lower, upper):
        u = tiles(src, p + off)
        uy = y_up(u)
        fy = [cy[p, :, tile(t)] * (uy[t] - u[t]) for t in range(LT)]
        fd = y_down(fy)
        out = []
        for t in range(LT):
            fz = cz[p, :, tile(t)] * (pltpu.roll(u[t], BLK - 1, 1) - u[t])
            new = cd[p, :, tile(t)] * u[t] + ((fy[t] - fd[t]) + (fz - pltpu.roll(fz, 1, 1)))
            if upper:
                new = new + cx[p + 1, :, tile(t)] * (src[p + 1 + off, :, tile(t)] - u[t])
            if lower:
                new = new - cx[p, :, tile(t)] * (u[t] - src[p - 1 + off, :, tile(t)])
            out.append(new)
        return out

    for copy in loads:
        copy.wait()
    for copy in smalls:
        copy.wait()

    for p in (0, PLANES - 1):
        bring(p)

    pl.semaphore_wait(bar, NYR - 1 + G - 1 + G * has_up.astype(jnp.int32) + G * has_dn.astype(jnp.int32))

    ends = ((0, PLANES - 1, s_up, has_up), (1, 0, s_dn, has_dn))
    halo_field = [
        [
            remote(th.at[pl.ds(p * LT, LT)], thh.at[d], halo_s.at[d * 3], halo_r.at[d * 3], dest, e),
            remote(u0.at[p], uh.at[d], halo_s.at[d * 3 + 1], halo_r.at[d * 3 + 1], dest, e),
        ]
        for d, p, dest, _ in ends
    ]
    halo_part = [
        remote(ps.at[d], pr.at[d], halo_s.at[d * 3 + 2], halo_r.at[d * 3 + 2], dest, e) for d, p, dest, _ in ends
    ]
    for d, p, dest, has in ends:

        @pl.when(has)
        def _(d=d):
            for copy in halo_field[d]:
                copy.start()

    def pick(k, carry):
        upd[k] = th[pair_cells[0, k]]
        return carry

    loop(1, PLANES - 1, bring)
    lax.fori_loop(0, SLOTS, pick, 0, unroll=4)
    sub_copies = []
    for d, gg in enumerate(sub_g):
        sub_copies.append(
            remote(upd.at[pl.ds(gg * SPG, SPG)], thg.at[:, y, g], sub_s.at[d], sub_r.at[d], s, ens_of(gg, y))
        )
    for copy in sub_copies:
        copy.start()
    for i in range(SPG):
        thg[i, y, g] = upd[g * SPG + i]

    for p in (0, 1, PLANES - 2, PLANES - 1):
        viscosity(p)
    for p in (0, PLANES - 1):
        coefficients(p)
    face(1)
    face(PLANES - 1)
    put(ps, partial(u0, 0, PLANES - 1, True, False), 0)
    put(ps, partial(u0, 0, 0, False, True), 1)
    for d, p, dest, has in ends:

        @pl.when(has)
        def _(d=d):
            halo_part[d].start()

    right, left = ens_of(g, (y + 1) % NYR), ens_of(g, (y + NYR - 1) % NYR)
    half = SPG // 2

    def ring(step):
        a, b = (y + NYR - step) % NYR, (y + step) % NYR
        if step < 3:
            src_r, src_l = thg.at[:, a], thg.at[:, b]
        else:
            src_r, src_l = thg.at[pl.ds(0, half), a], thg.at[pl.ds(half, half), b]
        return [
            remote(src_r, src_r, ring_s.at[step * 2], ring_r.at[step * 2], s, right),
            remote(src_l, src_l, ring_s.at[step * 2 + 1], ring_r.at[step * 2 + 1], s, left),
        ]

    rings = [ring(step) for step in range(4)]

    loop(2, PLANES - 2, viscosity)
    for copy in sub_copies:
        copy.wait_recv()
    for copy in rings[0]:
        copy.start()
    loop(1, PLANES - 1, coefficients)
    loop(2, PLANES - 1, face)

    def first(p):
        put(u1, partial(u0, 0, p, True, True), p + 1)

    def second(p):
        for t, value in enumerate(partial(u1, 1, p, True, True)):
            u2[p * LT + t] = value

    loop(1, PLANES - 1, first)
    loop(2, PLANES - 2, second)
    for copy in rings[0]:
        copy.wait_recv()
    for copy in rings[1]:
        copy.start()

    for d, p, dest, has in ends:

        @pl.when(jnp.logical_not((has_dn, has_up)[d]))
        def _(d=d):
            uh[d] = jnp.zeros_like(uh[d])
            thh[d] = jnp.zeros_like(thh[d])
            pr[d] = jnp.zeros_like(pr[d])

    for d, p, dest, has in ends:

        @pl.when((has_dn, has_up)[d])
        def _(d=d):
            for copy in halo_field[d]:
                copy.wait_recv()
            halo_part[d].wait_recv()

    keep_dn = has_dn.astype(F32)
    keep_up = has_up.astype(F32)
    for t in range(LT):
        w = (slice(None), tile(t))
        face_lo = COEF * (jnp.exp(thh[0, t]) + vv[(0, *w)])
        flux = face_lo * (u0[(0, *w)] - uh[(0, *w)])
        cx[(0, *w)] = face_lo
        u1[(0, *w)] = (pr[(0, *w)] + flux) * keep_dn
        u1[(1, *w)] = ps[(1, *w)] - flux
        face_hi = COEF * (jnp.exp(thh[1, t]) + vv[(PLANES - 1, *w)])
        flux = face_hi * (uh[(1, *w)] - u0[(PLANES - 1, *w)])
        cx[(PLANES, *w)] = face_hi
        u1[(PLANES + 1, *w)] = (pr[(1, *w)] - flux) * keep_up
        u1[(PLANES, *w)] = ps[(0, *w)] + flux
    loop(0, 2, second)
    loop(PLANES - 2, PLANES, second)

    def probe(i, accs):
        new = []
        for b in range(2):
            cell = cells[b * BLK + i]
            row = u2[cell >> 7]
            one = jnp.sum(jnp.where(lane == (cell & (BLK - 1)), row, 0.0), axis=1, keepdims=True)
            new.append(jnp.where(lane == i, one, accs[b]))
        return tuple(new)

    zero = jnp.zeros((MEM, BLK), F32)
    pred = lax.fori_loop(0, BLK, probe, (zero, zero), unroll=4)
    for b in range(2):
        agb[y, g, :, tile(b)] = pred[b]

    order = [4, 3, 5, 2, 6, 1, 7]
    ag1 = [
        remote(agb.at[y, g], agb.at[y, g], ag1_s.at[d - 1], ag1_r.at[d - 1], s, ens_of(g, (y + d) % NYR)) for d in order
    ]
    for copy in ag1:
        copy.start()
    for copy in rings[1]:
        copy.wait_recv()
    for copy in rings[2]:
        copy.start()

    def back(p):
        for t in range(LT):
            ost[t, pl.ds(p, MEM, PLANES), :] = u2[p * LT + t]

    loop(0, PLANES, back)
    stores = [pltpu.make_async_copy(ost.at[t], prior_hbm.at[:, tile(t)], out_sem.at[t]) for t in range(LT)]
    for copy in stores:
        copy.start()
    scaled = [
        (obs_ref[:, tile(b)] + noise_ref[:, tile(b)] - pred[b]) / var_ref[:, tile(b)] for b in range(2)
    ]
    for copy in ag1:
        copy.wait_recv()
    ag2 = [
        remote(agb.at[:, g], agb.at[:, g], ag2_s.at[d], ag2_r.at[d], s, ens_of(gg, y)) for d, gg in enumerate(sub_g)
    ]
    for copy in ag2:
        copy.start()
    for copy in ag2:
        copy.wait_recv()

    everyone = agb[...].reshape(ALL, 2 * BLK)
    anom[...] = everyone - jnp.sum(everyone, axis=0, keepdims=True) * (1.0 / ALL)
    for b in range(2):
        part = dot(scaled[b], anom[:, tile(b)], NT)
        a_own[b] = part
        a_win[2 + b] = part
    ax = [
        remote(a_own, a_win.at[pl.ds(0, 2)], ax_s.at[0], ax_r.at[0], s_up, e),
        remote(a_own, a_win.at[pl.ds(4, 2)], ax_s.at[1], ax_r.at[1], s_dn, e),
    ]
    for d, has in ((0, has_up), (1, has_dn)):

        @pl.when(has)
        def _(d=d):
            ax[d].start()

    for copy in rings[2]:
        copy.wait_recv()
    for copy in rings[3]:
        copy.start()

    for d, has in ((0, has_dn), (1, has_up)):

        @pl.when(jnp.logical_not(has))
        def _(d=d):
            for b in range(2):
                a_win[4 * d + b] = jnp.zeros((MEM, ALL), F32)
                k_win[4 * d + b] = jnp.zeros((G, MEM, ALL), F32)

        @pl.when(has)
        def _(d=d):
            ax[d].wait_recv()

    for b in range(2):
        mix = probe_taper[0, b, 0].astype(F32) * a_win[0]
        for j in range(1, 6):
            mix = mix + probe_taper[0, b, j].astype(F32) * a_win[j]
        corr = dot(mix * (1.0 / 256.0 / (ALL - 1)), anom[:, tile(b)], NN)
        gain = scaled[b] - corr / var_ref[:, tile(b)]
        gain_out[:, tile(b)] = gain
        kk = dot(gain, anom[:, tile(b)], NT)
        k_own[b] = kk
        k_win[2 + b, g] = kk
    kx_up = [remote(k_own, k_win.at[pl.ds(0, 2), g], kx_s.at[gg], kx_r.at[g], s_up, ens_of(gg, y)) for gg in range(G)]
    kx_dn = [
        remote(k_own, k_win.at[pl.ds(4, 2), g], kx_s.at[G + gg], kx_r.at[G + g], s_dn, ens_of(gg, y))
        for gg in range(G)
    ]
    kx_own = [
        remote(k_own, k_win.at[pl.ds(2, 2), g], kx_s.at[2 * G + d], kx_r.at[2 * G + d], s, ens_of(gg, y))
        for d, gg in enumerate(sub_g)
    ]

    @pl.when(has_up)
    def _():
        for copy in kx_up:
            copy.start()

    @pl.when(has_dn)
    def _():
        for copy in kx_dn:
            copy.start()

    for copy in kx_own:
        copy.start()
    for copy in rings[3]:
        copy.wait_recv()
    for copy in kx_own:
        copy.wait_recv()
    for base, has in ((0, has_dn), (G, has_up)):

        @pl.when(has)
        def _(base=base):
            for gg in range(G):
                remote(
                    k_own, k_win.at[pl.ds(0, 2), g], kx_s.at[0], kx_r.at[base + gg], s, ens_of(gg, y)
                ).wait_recv()

    for i in range(SPG):
        k = g * SPG + i
        left_side = k_win[pair_probes[0, k]].reshape(G * MEM, ALL)
        us[i] = dot(left_side, thg[i].reshape(ALL, BLK), NN).reshape(G, MEM, BLK)
    for copy in sub_copies:
        copy.wait_send()
    ux = [
        remote(us.at[:, gg], upd_out.at[pl.ds(g * SPG, SPG)], ux_s.at[d], ux_r.at[d], s, ens_of(gg, y))
        for d, gg in enumerate(sub_g)
    ]
    for copy in ux:
        copy.start()
    for i in range(SPG):
        upd_out[g * SPG + i] = us[i, g]

    for d, p, dest, has in ends:

        @pl.when(has)
        def _(d=d):
            for copy in halo_field[d]:
                copy.wait_send()
            halo_part[d].wait_send()
            ax[d].wait_send()
            for copy in (kx_up, kx_dn)[d]:
                copy.wait_send()

    for copy in [q for step in rings for q in step] + ag1 + ag2 + kx_own:
        copy.wait_send()
    for copy in stores:
        copy.wait()
    for copy in ux:
        copy.wait()


def tail_kernel(pair_cells, pair_taper, pair_counts, t_hbm, upd, post_out, st, sem_i, sem_o):
    loads = [pltpu.make_async_copy(t_hbm.at[:, tile(t)], st.at[t], sem_i.at[t]) for t in range(LT)]
    for copy in loads:
        copy.start()
    for copy in loads:
        copy.wait()

    def add(k, carry):
        b = pair_cells[0, k]
        w = jnp.where(k < pair_counts[0], pair_taper[0, k].astype(F32) * (1.0 / 256.0), 0.0) * (1.0 / (ALL - 1))
        rows = pl.ds(b // LT, MEM, PLANES)
        st[b % LT, rows, :] = st[b % LT, rows, :] + w * upd[k]
        return carry

    lax.fori_loop(0, SLOTS, add, 0)
    stores = [pltpu.make_async_copy(st.at[t], post_out.at[:, tile(t)], sem_o.at[t]) for t in range(LT)]
    for copy in stores:
        copy.start()
    for copy in stores:
        copy.wait()


def shards(u, theta, observed, obs_noise, obs_var, probe_cells, pair_cells, pair_probes, pair_taper, pair_counts, probe_taper):
    shape = u.shape
    rows, cols = shape[0] * shape[1], shape[2]
    u, theta = u.reshape(rows, cols), theta.reshape(rows, cols)
    any_ = pl.BlockSpec(memory_space=pl.ANY)
    vmem = pl.BlockSpec(memory_space=pltpu.VMEM)
    smem = pl.BlockSpec(memory_space=pltpu.SMEM)
    big = (PLANES, MEM, cols)
    dma = pltpu.SemaphoreType.DMA

    def buf(*dims):
        return pltpu.VMEM(dims, F32)

    prior, gain, upd = pl.pallas_call(
        main_kernel,
        name="assimilate",
        out_shape=(
            jax.ShapeDtypeStruct((rows, cols), F32),
            jax.ShapeDtypeStruct((MEM, 2 * BLK), F32),
            jax.ShapeDtypeStruct((SLOTS, MEM, BLK), F32),
        ),
        in_specs=[any_] * 5 + [smem] * 4,
        out_specs=(any_, vmem, vmem),
        scratch_shapes=[
            buf(LT, rows, BLK), buf(LT, rows, BLK), buf(*big), buf(PLANES * LT, MEM, BLK), buf(*big),
            buf(PLANES + 1, MEM, cols), buf(*big), buf(*big), buf(*big),
            buf(2, MEM, cols), buf(2, LT, MEM, BLK), buf(2, MEM, cols), buf(2, MEM, cols),
            buf(PLANES + 2, MEM, cols), buf(PLANES * LT, MEM, BLK), buf(LT, rows, BLK),
            buf(SPG, NYR, G, MEM, BLK), buf(NYR, G, MEM, 2 * BLK), buf(ALL, 2 * BLK),
            buf(2, MEM, ALL), buf(6, MEM, ALL), buf(2, MEM, ALL), buf(6, G, MEM, ALL),
            buf(SPG, G, MEM, BLK), buf(SLOTS, MEM, BLK),
            dma((2 * LT,)), dma((LT,)), dma((6,)), dma((6,)), dma((3,)), dma((3,)), dma((8,)), dma((8,)),
            dma((7,)), dma((7,)), dma((3,)), dma((3,)), dma((2,)), dma((2,)),
            dma((11,)), dma((11,)), dma((3,)), dma((3,)),
            buf(1, 2 * BLK), buf(MEM, 2 * BLK), buf(1, 2 * BLK), dma((3,)),
        ],
        compiler_params=pltpu.CompilerParams(
            collective_id=0, has_side_effects=True
        ),
    )(
        u, theta, observed.reshape(1, -1), obs_noise, obs_var.reshape(1, -1), probe_cells, pair_cells, pair_probes,
        probe_taper,
    )
    post = pl.pallas_call(
        tail_kernel,
        name="tail",
        out_shape=jax.ShapeDtypeStruct((rows, cols), F32),
        in_specs=[smem, smem, smem, any_, vmem],
        out_specs=any_,
        scratch_shapes=[buf(LT, rows, BLK), dma((LT,)), dma((LT,))],
    )(pair_cells, pair_taper, pair_counts, theta, upd)
    return prior.reshape(shape), post.reshape(shape), gain


def solution(mesh):
    return jax.shard_map(
        shards,
        mesh=mesh,
        in_specs=(
            P("ens", "space", None), P("ens", "space", None), P("space"), P("ens", "space"), P("space"), P("space"),
            P("space", None), P("space", None), P("space", None), P("space"), P("space", None, None),
        ),
        out_specs=(P("ens", "space", None), P("ens", "space", None), P("ens", "space")),
        check_vma=False,
    )
```

```python
import functools

import jax
import jax.numpy as jnp
from jax import lax
from jax.experimental import pallas as pl
from jax.experimental.pallas import tpu as pltpu
from jax.sharding import PartitionSpec as P

BLK = 128
NZ = 64
DT_STEP = 0.08
COEF = 0.5 * DT_STEP

NS = 16
NYR = 8
G = 4
PLANES = 16
LT = 16
MEM = 8
ALL = 256
SLOTS = 32
SPG = SLOTS // G

MESH = pl.DeviceIdType.MESH
HIGHEST = lax.Precision.HIGHEST
F32 = jnp.float32


def dot(a, b, dims):
    return lax.dot_general(a, b, (dims, ((), ())), precision=HIGHEST, preferred_element_type=F32)


NN = ((1,), (0,))
NT = ((1,), (1,))


def tile(t):
    return slice(t * BLK, (t + 1) * BLK)


def tiles(ref, *where):
    return [ref[(*where, slice(None), tile(t))] for t in range(LT)]


def put(ref, values, *where):
    for t in range(LT):
        ref[(*where, slice(None), tile(t))] = values[t]


def main_kernel(
    u_hbm, t_hbm, *refs
):
    smalls_hbm, refs = refs[:7], refs[7:]
    (
        ost, tst, gain_out, upd_out,
        ust, u0, th, vv, cx, cy, cz, cd, uh, thh, ps, pr, u1, u2,
        thg, agb, scw, anom, a_part, a_win, k_own, k_win, us, upd,
        obs_ref, noise_ref, var_ref, cells, pair_cells, pair_probes, probe_taper,
        in_sem, small_sem, halo_s, halo_r, sub_s, sub_r, ring_s, ring_r, ag1_s, ag1_r, ag2_s, ag2_r, sc_s, sc_r,
        ax_s, ax_r, kx_s, kx_r, ux_s, ux_r,
    ) = refs
    s = lax.axis_index("space")
    e = lax.axis_index("ens")
    xl, y, c = e // (2 * NYR), (e // 2) % NYR, e % 2
    g = xl * 2 + c
    has_up, has_dn = s < NS - 1, s > 0
    s_up, s_dn = jnp.minimum(s + 1, NS - 1), jnp.maximum(s - 1, 0)

    def ens_of(gg, yy):
        return (gg // 2) * (2 * NYR) + yy * 2 + gg % 2

    def remote(src, dst, ss, rs, space, ens):
        return pltpu.make_async_remote_copy(
            src_ref=src, dst_ref=dst, send_sem=ss, recv_sem=rs, device_id=(space, ens), device_id_type=MESH
        )

    sub_g = [(g + d) % G for d in range(1, G)]

    loads = []
    for k, (src, dst) in enumerate(((t_hbm, tst), (u_hbm, ust))):
        for t in range(LT):
            loads.append(pltpu.make_async_copy(src.at[:, tile(t)], dst.at[t], in_sem.at[k * LT + t]))
    for copy in loads:
        copy.start()
    smalls_vmem = (obs_ref, noise_ref, var_ref, cells, pair_cells, pair_probes, probe_taper)
    smalls = [pltpu.make_async_copy(a, b, small_sem.at[i]) for i, (a, b) in enumerate(zip(smalls_hbm, smalls_vmem))]
    for copy in smalls:
        copy.start()

    bar = pltpu.get_barrier_semaphore()
    for d in range(1, NYR):
        pl.semaphore_signal(bar, 1, device_id=(s, ens_of(g, (y + d) % NYR)), device_id_type=MESH)
    for gg in sub_g:
        pl.semaphore_signal(bar, 1, device_id=(s, ens_of(gg, y)), device_id_type=MESH)

    @pl.when(has_up)
    def _():
        for gg in range(G):
            pl.semaphore_signal(bar, 1, device_id=(s_up, ens_of(gg, y)), device_id_type=MESH)

    @pl.when(has_dn)
    def _():
        for gg in range(G):
            pl.semaphore_signal(bar, 1, device_id=(s_dn, ens_of(gg, y)), device_id_type=MESH)

    lane = lax.broadcasted_iota(jnp.int32, (MEM, BLK), 1)
    low = lane < NZ
    height = lane % NZ
    top = height == NZ - 1
    wall = (height == 0) | top

    def bring(p):
        for t in range(LT):
            rows = pl.ds(p, MEM, PLANES)
            th[p * LT + t] = tst[t, rows, :]
            u0[p, :, tile(t)] = ust[t, rows, :]

    def viscosity(p):
        for t in range(LT):
            vv[p, :, tile(t)] = jnp.exp(th[p * LT + t])

    def loop(lo, hi, fn):
        def body(p, carry):
            fn(p)
            return carry

        lax.fori_loop(lo, hi, body, 0)

    def coefficients(p):
        def load(t):
            v = vv[p, :, tile(t % LT)]
            return v, pltpu.roll(v, NZ, 1)

        here = load(0)
        for t in range(LT):
            beside = load(t + 1)
            v = here[0]
            cy[p, :, tile(t)] = COEF * (v + jnp.where(low, here[1], beside[1]))
            cz[p, :, tile(t)] = jnp.where(top, 0.0, COEF * (v + pltpu.roll(v, BLK - 1, 1)))
            cd[p, :, tile(t)] = 1.0 - jnp.where(wall, COEF * (v + 1.0), 0.0)
            here = beside

    def face(p):
        for t in range(LT):
            cx[p, :, tile(t)] = COEF * (vv[p - 1, :, tile(t)] + vv[p, :, tile(t)])

    def step(src, off, p, lower, upper, emit):
        def load(t):
            v = src[p + off, :, tile(t % LT)]
            return v, pltpu.roll(v, NZ, 1)

        def flux_y(t, here, beside):
            f = cy[p, :, tile(t)] * (jnp.where(low, here[1], beside[1]) - here[0])
            return f, pltpu.roll(f, NZ, 1)

        here = first_one = load(0)
        before = last = load(LT - 1)
        f_prev = f_last = flux_y(LT - 1, last, first_one)
        for t in range(LT):
            beside = load(t + 1)
            f = flux_y(t, here, beside) if t < LT - 1 else f_last
            v = here[0]
            fz = cz[p, :, tile(t)] * (pltpu.roll(v, BLK - 1, 1) - v)
            new = cd[p, :, tile(t)] * v + ((f[0] - jnp.where(low, f_prev[1], f[1])) + (fz - pltpu.roll(fz, 1, 1)))
            if upper:
                new = new + cx[p + 1, :, tile(t)] * (src[p + 1 + off, :, tile(t)] - v)
            if lower:
                new = new - cx[p, :, tile(t)] * (v - src[p - 1 + off, :, tile(t)])
            emit(t, new)
            here, f_prev = beside, f

    def into(ref, *where):
        def emit(t, value):
            ref[(*where, slice(None), tile(t))] = value

        return emit

    for copy in loads:
        copy.wait()

    for p in (0, PLANES - 1):
        bring(p)

    pl.semaphore_wait(bar, NYR - 1 + G - 1 + G * has_up.astype(jnp.int32) + G * has_dn.astype(jnp.int32))

    ends = ((0, PLANES - 1, s_up, has_up), (1, 0, s_dn, has_dn))
    halo_field = [
        [
            remote(th.at[pl.ds(p * LT, LT)], thh.at[d], halo_s.at[d * 3], halo_r.at[d * 3], dest, e),
            remote(u0.at[p], uh.at[d], halo_s.at[d * 3 + 1], halo_r.at[d * 3 + 1], dest, e),
        ]
        for d, p, dest, _ in ends
    ]
    halo_part = [
        remote(ps.at[d], pr.at[d], halo_s.at[d * 3 + 2], halo_r.at[d * 3 + 2], dest, e) for d, p, dest, _ in ends
    ]
    for d, p, dest, has in ends:

        @pl.when(has)
        def _(d=d):
            for copy in halo_field[d]:
                copy.start()

    for p in (1, PLANES - 2):
        bring(p)
    for p in (0, 1, PLANES - 2, PLANES - 1):
        viscosity(p)
    for p in (0, PLANES - 1):
        coefficients(p)
    face(1)
    face(PLANES - 1)
    step(u0, 0, PLANES - 1, True, False, into(ps, 0))
    step(u0, 0, 0, False, True, into(ps, 1))
    for d, p, dest, has in ends:

        @pl.when(has)
        def _(d=d):
            halo_part[d].start()

    def pick(k, carry):
        upd[k] = th[pair_cells[0, k]]
        return carry

    loop(2, PLANES - 2, bring)
    for copy in smalls:
        copy.wait()
    lax.fori_loop(0, SLOTS, pick, 0, unroll=4)
    sub_copies = []
    for d, gg in enumerate(sub_g):
        sub_copies.append(
            remote(upd.at[pl.ds(gg * SPG, SPG)], thg.at[:, y, g], sub_s.at[d], sub_r.at[d], s, ens_of(gg, y))
        )
    for copy in sub_copies:
        copy.start()
    for i in range(SPG):
        thg[i, y, g] = upd[g * SPG + i]

    right, left = ens_of(g, (y + 1) % NYR), ens_of(g, (y + NYR - 1) % NYR)
    half = SPG // 2

    def ring(n):
        a, b = (y + NYR - n) % NYR, (y + n) % NYR
        if n < 3:
            src_r, src_l = thg.at[:, a], thg.at[:, b]
        else:
            src_r, src_l = thg.at[pl.ds(0, half), a], thg.at[pl.ds(half, half), b]
        return [
            remote(src_r, src_r, ring_s.at[n * 2], ring_r.at[n * 2], s, right),
            remote(src_l, src_l, ring_s.at[n * 2 + 1], ring_r.at[n * 2 + 1], s, left),
        ]

    rings = [ring(n) for n in range(4)]

    loop(2, PLANES - 2, viscosity)
    for copy in sub_copies:
        copy.wait_recv()
    for copy in rings[0]:
        copy.start()
    loop(1, PLANES - 1, coefficients)
    loop(2, PLANES - 1, face)

    def first(p):
        step(u0, 0, p, True, True, into(u1, p + 1))

    def second(p):
        def emit(t, value):
            u2[p * LT + t] = value

        step(u1, 1, p, True, True, emit)

    loop(1, PLANES - 1, first)
    loop(2, PLANES - 2, second)
    for copy in rings[0]:
        copy.wait_recv()
    for copy in rings[1]:
        copy.start()

    for d, p, dest, has in ends:

        @pl.when(jnp.logical_not((has_dn, has_up)[d]))
        def _(d=d):
            uh[d] = jnp.zeros_like(uh[d])
            thh[d] = jnp.zeros_like(thh[d])
            pr[d] = jnp.zeros_like(pr[d])

    for d, p, dest, has in ends:

        @pl.when((has_dn, has_up)[d])
        def _(d=d):
            for copy in halo_field[d]:
                copy.wait_recv()
            halo_part[d].wait_recv()

    keep_dn = has_dn.astype(F32)
    keep_up = has_up.astype(F32)
    for t in range(LT):
        w = (slice(None), tile(t))
        face_lo = COEF * (jnp.exp(thh[0, t]) + vv[(0, *w)])
        flux = face_lo * (u0[(0, *w)] - uh[(0, *w)])
        cx[(0, *w)] = face_lo
        u1[(0, *w)] = (pr[(0, *w)] + flux) * keep_dn
        u1[(1, *w)] = ps[(1, *w)] - flux
        face_hi = COEF * (jnp.exp(thh[1, t]) + vv[(PLANES - 1, *w)])
        flux = face_hi * (uh[(1, *w)] - u0[(PLANES - 1, *w)])
        cx[(PLANES, *w)] = face_hi
        u1[(PLANES + 1, *w)] = (pr[(1, *w)] - flux) * keep_up
        u1[(PLANES, *w)] = ps[(0, *w)] + flux
    loop(0, 2, second)
    loop(PLANES - 2, PLANES, second)

    def probe(i, accs):
        new = []
        for b in range(2):
            cell = cells[b * BLK + i]
            row = u2[cell >> 7]
            one = jnp.sum(jnp.where(lane == (cell & (BLK - 1)), row, 0.0), axis=1, keepdims=True)
            new.append(jnp.where(lane == i, one, accs[b]))
        return tuple(new)

    zero = jnp.zeros((MEM, BLK), F32)
    pred = lax.fori_loop(0, BLK, probe, (zero, zero), unroll=16)
    for b in range(2):
        agb[g, y, :, tile(b)] = pred[b]

    def onward(i, yy):
        return [
            remote(agb.at[g, yy], agb.at[g, yy], ag2_s.at[d * NYR + i], ag2_r.at[d * NYR + i], s, ens_of(gg, y))
            for d, gg in enumerate(sub_g)
        ]

    order = [4, 3, 5, 2, 6, 1, 7]
    ag1 = {
        d: remote(agb.at[g, y], agb.at[g, y], ag1_s.at[d - 1], ag1_r.at[d - 1], s, ens_of(g, (y + d) % NYR))
        for d in order
    }
    for d in order:
        ag1[d].start()
    scaled = [
        (obs_ref[:, tile(b)] + noise_ref[:, tile(b)] - pred[b]) / var_ref[:, tile(b)] for b in range(2)
    ]
    for b in range(2):
        scw[g, :, tile(b)] = scaled[b]
    sc = [
        remote(scw.at[g], scw.at[g], sc_s.at[d], sc_r.at[d], s, ens_of(gg, y)) for d, gg in enumerate(sub_g)
    ]
    for copy in sc:
        copy.start()
    ag2 = onward(0, y)
    for copy in ag2:
        copy.start()

    def back(p):
        for t in range(LT):
            ost[t, pl.ds(p, MEM, PLANES), :] = u2[p * LT + t]

    loop(0, PLANES, back)
    for copy in rings[1]:
        copy.wait_recv()
    for d in reversed(order):
        ag1[d].wait_recv()
        more = onward(d, (y + NYR - d) % NYR)
        for copy in more:
            copy.start()
        ag2 = ag2 + more
    for copy in rings[2]:
        copy.start()
    for copy in sc:
        copy.wait_recv()

    own_class = agb[g].reshape(NYR * MEM, 2 * BLK)
    wide = scw[...].reshape(G * MEM, 2 * BLK)
    half_a = [dot(wide[:, tile(b)], own_class[:, tile(b)], NT) for b in range(2)]
    a_part[...] = jnp.concatenate(half_a, axis=1).reshape(G, MEM, BLK)
    a_win[1, g] = a_part[g]
    ax_up = [remote(a_part.at[gg], a_win.at[0, g], ax_s.at[gg], ax_r.at[g], s_up, ens_of(gg, y)) for gg in range(G)]
    ax_dn = [
        remote(a_part.at[gg], a_win.at[2, g], ax_s.at[G + gg], ax_r.at[G + g], s_dn, ens_of(gg, y)) for gg in range(G)
    ]
    ax_own = [
        remote(a_part.at[gg], a_win.at[1, g], ax_s.at[2 * G + d], ax_r.at[2 * G + d], s, ens_of(gg, y))
        for d, gg in enumerate(sub_g)
    ]

    @pl.when(has_up)
    def _():
        for copy in ax_up:
            copy.start()

    @pl.when(has_dn)
    def _():
        for copy in ax_dn:
            copy.start()

    for copy in ax_own:
        copy.start()
    for d, has in ((0, has_dn), (1, has_up)):

        @pl.when(jnp.logical_not(has))
        def _(d=d):
            a_win[2 * d] = jnp.zeros((G, MEM, BLK), F32)
            for b in range(2):
                k_win[4 * d + b] = jnp.zeros((G, MEM, ALL), F32)

    for copy in ag2:
        copy.wait_recv()
    everyone = agb[...].reshape(ALL, 2 * BLK)
    anom[...] = everyone - jnp.sum(everyone, axis=0, keepdims=True) * (1.0 / ALL)
    for copy in rings[2]:
        copy.wait_recv()
    for copy in rings[3]:
        copy.start()
    for copy in ax_own:
        copy.wait_recv()
    for base, has in ((0, has_dn), (G, has_up)):

        @pl.when(has)
        def _(base=base):
            for gg in range(G):
                remote(a_part.at[0], a_win.at[0, g], ax_s.at[0], ax_r.at[base + gg], s, ens_of(gg, y)).wait_recv()

    for b in range(2):
        mixed = []
        for gg in range(G):
            mix = None
            for n in range(3):
                level = jnp.where(low, probe_taper[0, b, 2 * n].astype(F32), probe_taper[0, b, 2 * n + 1].astype(F32))
                term = a_win[n, gg] * level
                mix = term if mix is None else mix + term
            mixed.append(mix + pltpu.roll(mix, NZ, 1))
        mix = jnp.concatenate([jnp.where(low, mixed[q], mixed[q + 1]) for q in range(0, G, 2)], axis=1)
        corr = dot(mix * (1.0 / 256.0 / (ALL - 1)), anom[:, tile(b)], NN)
        gain = scaled[b] - corr / var_ref[:, tile(b)]
        gain_out[:, tile(b)] = gain
        kk = dot(gain, anom[:, tile(b)], NT)
        k_own[b] = kk
        k_win[2 + b, g] = kk
    kx_up = [remote(k_own, k_win.at[pl.ds(0, 2), g], kx_s.at[gg], kx_r.at[g], s_up, ens_of(gg, y)) for gg in range(G)]
    kx_dn = [
        remote(k_own, k_win.at[pl.ds(4, 2), g], kx_s.at[G + gg], kx_r.at[G + g], s_dn, ens_of(gg, y))
        for gg in range(G)
    ]
    kx_own = [
        remote(k_own, k_win.at[pl.ds(2, 2), g], kx_s.at[2 * G + d], kx_r.at[2 * G + d], s, ens_of(gg, y))
        for d, gg in enumerate(sub_g)
    ]

    @pl.when(has_up)
    def _():
        for copy in kx_up:
            copy.start()

    @pl.when(has_dn)
    def _():
        for copy in kx_dn:
            copy.start()

    for copy in kx_own:
        copy.start()
    for copy in rings[3]:
        copy.wait_recv()
    for copy in kx_own:
        copy.wait_recv()
    for base, has in ((0, has_dn), (G, has_up)):

        @pl.when(has)
        def _(base=base):
            for gg in range(G):
                remote(
                    k_own, k_win.at[pl.ds(0, 2), g], kx_s.at[0], kx_r.at[base + gg], s, ens_of(gg, y)
                ).wait_recv()

    for i in range(SPG):
        k = g * SPG + i
        left_side = k_win[pair_probes[0, k]].reshape(G * MEM, ALL)
        fields = jnp.concatenate([thg[i, :, gg].reshape(NYR * MEM, BLK) for gg in range(G)], axis=0)
        us[i] = dot(left_side, fields, NN).reshape(G, MEM, BLK)
    for copy in sub_copies:
        copy.wait_send()
    ux = [
        remote(us.at[:, gg], upd_out.at[pl.ds(g * SPG, SPG)], ux_s.at[d], ux_r.at[d], s, ens_of(gg, y))
        for d, gg in enumerate(sub_g)
    ]
    for copy in ux:
        copy.start()
    for i in range(SPG):
        upd_out[g * SPG + i] = us[i, g]

    for d, p, dest, has in ends:

        @pl.when(has)
        def _(d=d):
            for copy in halo_field[d]:
                copy.wait_send()
            halo_part[d].wait_send()
            for copy in (ax_up, ax_dn)[d] + (kx_up, kx_dn)[d]:
                copy.wait_send()

    for copy in [q for each in rings for q in each] + list(ag1.values()) + ag2 + sc + ax_own + kx_own:
        copy.wait_send()
    for copy in ux:
        copy.wait()


def tail_kernel(
    cells_hbm, taper_hbm, pair_counts, prior_st, theta_st, upd, gain_in, prior_out, post_out, gain_out, post_st,
    pair_cells, pair_taper, sem_i, sem_p, sem_o,
):
    smalls = [
        pltpu.make_async_copy(a, b, sem_i.at[i])
        for i, (a, b) in enumerate(((cells_hbm, pair_cells), (taper_hbm, pair_taper)))
    ]
    for copy in smalls:
        copy.start()
    stores = [pltpu.make_async_copy(prior_st.at[t], prior_out.at[:, tile(t)], sem_p.at[t]) for t in range(LT)]
    for copy in stores:
        copy.start()
    gain_out[...] = gain_in[...]
    for copy in smalls:
        copy.wait()

    def add(k, carry):
        b = pair_cells[0, k]
        w = jnp.where(k < pair_counts[0], pair_taper[0, k].astype(F32) * (1.0 / 256.0), 0.0) * (1.0 / (ALL - 1))
        rows = pl.ds(b // LT, MEM, PLANES)
        post_st[b % LT, rows, :] = post_st[b % LT, rows, :] + w * upd[k]
        return carry

    lax.fori_loop(0, SLOTS, add, 0)
    late = [pltpu.make_async_copy(post_st.at[t], post_out.at[:, tile(t)], sem_o.at[t]) for t in range(LT)]
    for copy in late:
        copy.start()
    for copy in stores + late:
        copy.wait()


def shards(u, theta, observed, obs_noise, obs_var, probe_cells, pair_cells, pair_probes, pair_taper, pair_counts, probe_taper):
    shape = u.shape
    rows, cols = shape[0] * shape[1], shape[2]
    u, theta = u.reshape(rows, cols), theta.reshape(rows, cols)
    hbm = pl.BlockSpec(memory_space=pltpu.HBM)
    vmem = pl.BlockSpec(memory_space=pltpu.VMEM)
    big = (PLANES, MEM, cols)
    staged = (LT, rows, BLK)
    flat = (PLANES * LT, MEM, BLK)
    dma = pltpu.SemaphoreType.DMA

    def buf(*dims):
        return pltpu.VMEM(dims, F32)

    def stay(x):
        return pltpu.with_memory_space_constraint(x, pltpu.HBM)

    def ints(*dims):
        return pltpu.SMEM(dims, jnp.int32)

    def arr(*dims):
        return jax.ShapeDtypeStruct(dims, F32)

    prior_st, theta_st, gain, upd = pl.pallas_call(
        main_kernel,
        name="assimilate",
        out_shape=(arr(*staged), arr(*staged), arr(MEM, 2 * BLK), arr(SLOTS, MEM, BLK)),
        in_specs=[hbm] * 9,
        out_specs=(vmem,) * 4,
        scratch_shapes=[
            buf(*staged), buf(*big), buf(*flat), buf(*big),
            buf(PLANES + 1, MEM, cols), buf(*big), buf(*big), buf(*big),
            buf(2, MEM, cols), buf(2, LT, MEM, BLK), buf(2, MEM, cols), buf(2, MEM, cols),
            buf(PLANES + 2, MEM, cols), buf(*flat),
            buf(SPG, NYR, G, MEM, BLK), buf(G, NYR, MEM, 2 * BLK), buf(G, MEM, 2 * BLK), buf(ALL, 2 * BLK),
            buf(G, MEM, BLK), buf(3, G, MEM, BLK), buf(2, MEM, ALL), buf(6, G, MEM, ALL),
            buf(SPG, G, MEM, BLK), buf(SLOTS, MEM, BLK),
            buf(1, 2 * BLK), buf(MEM, 2 * BLK), buf(1, 2 * BLK),
            ints(2 * BLK), ints(1, SLOTS), ints(1, SLOTS), ints(1, 2, 6),
            dma((2 * LT,)), dma((7,)), dma((6,)), dma((6,)), dma((3,)), dma((3,)), dma((8,)), dma((8,)),
            dma((7,)), dma((7,)), dma((24,)), dma((24,)), dma((3,)), dma((3,)),
            dma((11,)), dma((11,)), dma((11,)), dma((11,)), dma((3,)), dma((3,)),
        ],
        compiler_params=pltpu.CompilerParams(
            collective_id=0, has_side_effects=True, vmem_limit_bytes=28 * 1024 * 1024
        ),
    )(
        *map(
            stay,
            (
                u, theta, observed.reshape(1, -1), obs_noise, obs_var.reshape(1, -1), probe_cells, pair_cells,
                pair_probes, probe_taper,
            ),
        )
    )
    prior, post, gain, _ = pl.pallas_call(
        tail_kernel,
        name="tail",
        out_shape=(arr(rows, cols), arr(rows, cols), arr(MEM, 2 * BLK), arr(*staged)),
        in_specs=[hbm, hbm, pl.BlockSpec(memory_space=pltpu.SMEM)] + [vmem] * 4,
        out_specs=(hbm, hbm, vmem, vmem),
        input_output_aliases={4: 3},
        scratch_shapes=[
            ints(1, SLOTS), ints(1, SLOTS), dma((2,)), dma((LT,)), dma((LT,)),
        ],
        compiler_params=pltpu.CompilerParams(vmem_limit_bytes=16 * 1024 * 1024),
    )(stay(pair_cells), stay(pair_taper), pair_counts, prior_st, theta_st, upd, gain)
    return prior.reshape(shape), post.reshape(shape), gain


def solution(mesh):
    return jax.shard_map(
        shards,
        mesh=mesh,
        in_specs=(
            P("ens", "space", None), P("ens", "space", None), P("space"), P("ens", "space"), P("space"), P("space"),
            P("space", None), P("space", None), P("space", None), P("space"), P("space", None, None),
        ),
        out_specs=(P("ens", "space", None), P("ens", "space", None), P("ens", "space")),
        check_vma=False,
    )
```

```python
import functools

import jax
import jax.numpy as jnp
from jax import lax
from jax.experimental import pallas as pl
from jax.experimental.pallas import tpu as pltpu
from jax.sharding import PartitionSpec as P

BLK = 128
NZ = 64
DT_STEP = 0.08
COEF = 0.5 * DT_STEP

NS = 16
NYR = 8
G = 4
PLANES = 16
LT = 16
MEM = 8
ALL = 256
SLOTS = 32
SPG = SLOTS // G

MESH = pl.DeviceIdType.MESH
HIGHEST = lax.Precision.HIGHEST
F32 = jnp.float32


def dot(a, b, dims):
    return lax.dot_general(a, b, (dims, ((), ())), precision=HIGHEST, preferred_element_type=F32)


NN = ((1,), (0,))
NT = ((1,), (1,))


def tile(t):
    return slice(t * BLK, (t + 1) * BLK)


def tiles(ref, *where):
    return [ref[(*where, slice(None), tile(t))] for t in range(LT)]


def put(ref, values, *where):
    for t in range(LT):
        ref[(*where, slice(None), tile(t))] = values[t]


def main_kernel(
    u_hbm, t_hbm, *refs
):
    smalls_hbm, refs = refs[:7], refs[7:]
    (
        ost, tst, gain_out, upd_out,
        ust, u0, th, vv, cx, cy, cz, cd, uh, thh, ps, pr, u1, u2,
        thg, agb, scw, anom, a_part, a_win, k_own, k_win, us, upd,
        obs_ref, noise_ref, var_ref, cells, pair_cells, pair_probes, probe_taper,
        in_sem, small_sem, halo_s, halo_r, sub_s, sub_r, ring_s, ring_r, ag1_s, ag1_r, ag2_s, ag2_r, sc_s, sc_r,
        ax_s, ax_r, kx_s, kx_r, ux_s, ux_r,
    ) = refs
    s = lax.axis_index("space")
    e = lax.axis_index("ens")
    xl, y, c = e // (2 * NYR), (e // 2) % NYR, e % 2
    g = xl * 2 + c
    has_up, has_dn = s < NS - 1, s > 0
    s_up, s_dn = jnp.minimum(s + 1, NS - 1), jnp.maximum(s - 1, 0)

    def ens_of(gg, yy):
        return (gg // 2) * (2 * NYR) + yy * 2 + gg % 2

    def remote(src, dst, ss, rs, space, ens):
        return pltpu.make_async_remote_copy(
            src_ref=src, dst_ref=dst, send_sem=ss, recv_sem=rs, device_id=(space, ens), device_id_type=MESH
        )

    sub_g = [(g + d) % G for d in range(1, G)]

    loads = []
    for k, (src, dst) in enumerate(((t_hbm, tst), (u_hbm, ust))):
        for t in range(LT):
            loads.append(pltpu.make_async_copy(src.at[:, tile(t)], dst.at[t], in_sem.at[k * LT + t]))
    for copy in loads:
        copy.start()
    smalls_vmem = (obs_ref, noise_ref, var_ref, cells, pair_cells, pair_probes, probe_taper)
    smalls = [pltpu.make_async_copy(a, b, small_sem.at[i]) for i, (a, b) in enumerate(zip(smalls_hbm, smalls_vmem))]
    for copy in smalls:
        copy.start()

    bar = pltpu.get_barrier_semaphore()
    for d in range(1, NYR):
        pl.semaphore_signal(bar, 1, device_id=(s, ens_of(g, (y + d) % NYR)), device_id_type=MESH)
    for gg in sub_g:
        pl.semaphore_signal(bar, 1, device_id=(s, ens_of(gg, y)), device_id_type=MESH)

    @pl.when(has_up)
    def _():
        for gg in range(G):
            pl.semaphore_signal(bar, 1, device_id=(s_up, ens_of(gg, y)), device_id_type=MESH)

    @pl.when(has_dn)
    def _():
        for gg in range(G):
            pl.semaphore_signal(bar, 1, device_id=(s_dn, ens_of(gg, y)), device_id_type=MESH)

    lane = lax.broadcasted_iota(jnp.int32, (MEM, BLK), 1)
    low = lane < NZ
    height = lane % NZ
    top = height == NZ - 1
    wall = (height == 0) | top

    def bring_theta(p):
        for t in range(LT):
            th[p * LT + t] = tst[t, pl.ds(p, MEM, PLANES), :]

    def bring_u(p):
        for t in range(LT):
            u0[p, :, tile(t)] = ust[t, pl.ds(p, MEM, PLANES), :]

    def viscosity(p):
        for t in range(LT):
            vv[p, :, tile(t)] = jnp.exp(th[p * LT + t])

    def loop(lo, hi, fn, unroll=2):
        def body(p, carry):
            fn(p)
            return carry

        lax.fori_loop(lo, hi, body, 0, unroll=unroll)

    def coefficients(p):
        def load(t):
            v = vv[p, :, tile(t % LT)]
            return v, pltpu.roll(v, NZ, 1)

        here = load(0)
        for t in range(LT):
            beside = load(t + 1)
            v = here[0]
            cy[p, :, tile(t)] = COEF * (v + jnp.where(low, here[1], beside[1]))
            cz[p, :, tile(t)] = jnp.where(top, 0.0, COEF * (v + pltpu.roll(v, BLK - 1, 1)))
            cd[p, :, tile(t)] = 1.0 - jnp.where(wall, COEF * (v + 1.0), 0.0)
            here = beside

    def face(p):
        for t in range(LT):
            cx[p, :, tile(t)] = COEF * (vv[p - 1, :, tile(t)] + vv[p, :, tile(t)])

    def step(src, off, p, lower, upper, emit):
        def load(t):
            v = src[p + off, :, tile(t % LT)]
            return v, pltpu.roll(v, NZ, 1)

        def flux_y(t, here, beside):
            f = cy[p, :, tile(t)] * (jnp.where(low, here[1], beside[1]) - here[0])
            return f, pltpu.roll(f, NZ, 1)

        here = first_one = load(0)
        before = last = load(LT - 1)
        f_prev = f_last = flux_y(LT - 1, last, first_one)
        for t in range(LT):
            beside = load(t + 1)
            f = flux_y(t, here, beside) if t < LT - 1 else f_last
            v = here[0]
            fz = cz[p, :, tile(t)] * (pltpu.roll(v, BLK - 1, 1) - v)
            new = cd[p, :, tile(t)] * v + ((f[0] - jnp.where(low, f_prev[1], f[1])) + (fz - pltpu.roll(fz, 1, 1)))
            if upper:
                new = new + cx[p + 1, :, tile(t)] * (src[p + 1 + off, :, tile(t)] - v)
            if lower:
                new = new - cx[p, :, tile(t)] * (v - src[p - 1 + off, :, tile(t)])
            emit(t, new)
            here, f_prev = beside, f

    def into(ref, *where):
        def emit(t, value):
            ref[(*where, slice(None), tile(t))] = value

        return emit

    for copy in loads[:LT] + smalls:
        copy.wait()
    loop(0, PLANES, bring_theta)

    def pick(k, carry):
        upd[k] = th[pair_cells[0, k]]
        return carry

    lax.fori_loop(0, SLOTS, pick, 0, unroll=4)
    thg[y, g] = upd[pl.ds(g * SPG, SPG)]
    sub_copies = [
        remote(upd.at[pl.ds(gg * SPG, SPG)], thg.at[y, g], sub_s.at[d], sub_r.at[d], s, ens_of(gg, y))
        for d, gg in enumerate(sub_g)
    ]

    rim = (0, 1, PLANES - 2, PLANES - 1)
    for p in rim:
        viscosity(p)
    for p in (0, PLANES - 1):
        coefficients(p)
    face(1)
    face(PLANES - 1)
    for copy in loads[LT:]:
        copy.wait()
    for p in rim:
        bring_u(p)
    step(u0, 0, PLANES - 1, True, False, into(ps, 0))
    step(u0, 0, 0, False, True, into(ps, 1))

    ends = ((0, PLANES - 1, s_up, has_up), (1, 0, s_dn, has_dn))
    halo = [
        [
            remote(th.at[pl.ds(p * LT, LT)], thh.at[d], halo_s.at[d * 3], halo_r.at[d * 3], dest, e),
            remote(u0.at[p], uh.at[d], halo_s.at[d * 3 + 1], halo_r.at[d * 3 + 1], dest, e),
            remote(ps.at[d], pr.at[d], halo_s.at[d * 3 + 2], halo_r.at[d * 3 + 2], dest, e),
        ]
        for d, p, dest, _ in ends
    ]
    pl.semaphore_wait(bar, NYR - 1 + G - 1 + G * has_up.astype(jnp.int32) + G * has_dn.astype(jnp.int32))
    for copy in sub_copies:
        copy.start()
    for d, p, dest, has in ends:

        @pl.when(has)
        def _(d=d):
            for copy in halo[d]:
                copy.start()

    right, left = ens_of(g, (y + 1) % NYR), ens_of(g, (y + NYR - 1) % NYR)
    half = G // 2

    def ring(n):
        a, b = (y + NYR - n) % NYR, (y + n) % NYR
        if n < 3:
            src_r, src_l = thg.at[a], thg.at[b]
        else:
            src_r, src_l = thg.at[a, pl.ds(0, half)], thg.at[b, pl.ds(half, half)]
        return [
            remote(src_r, src_r, ring_s.at[n * 2], ring_r.at[n * 2], s, right),
            remote(src_l, src_l, ring_s.at[n * 2 + 1], ring_r.at[n * 2 + 1], s, left),
        ]

    rings = [ring(n) for n in range(4)]

    loop(2, PLANES - 2, viscosity)
    loop(2, PLANES - 2, bring_u)
    loop(1, PLANES - 1, coefficients)
    loop(2, PLANES - 1, face, 1)

    def first(p):
        step(u0, 0, p, True, True, into(u1, p + 1))

    def second(p):
        def emit(t, value):
            u2[p * LT + t] = value

        step(u1, 1, p, True, True, emit)

    loop(1, PLANES - 1, first)
    for copy in sub_copies:
        copy.wait_recv()
    for copy in rings[0]:
        copy.start()
    loop(2, PLANES - 2, second)

    for d, p, dest, has in ends:

        @pl.when(jnp.logical_not((has_dn, has_up)[d]))
        def _(d=d):
            uh[d] = jnp.zeros_like(uh[d])
            thh[d] = jnp.zeros_like(thh[d])
            pr[d] = jnp.zeros_like(pr[d])

    for d, p, dest, has in ends:

        @pl.when((has_dn, has_up)[d])
        def _(d=d):
            for copy in halo[d]:
                copy.wait_recv()

    keep_dn = has_dn.astype(F32)
    keep_up = has_up.astype(F32)
    for t in range(LT):
        w = (slice(None), tile(t))
        face_lo = COEF * (jnp.exp(thh[0, t]) + vv[(0, *w)])
        flux = face_lo * (u0[(0, *w)] - uh[(0, *w)])
        cx[(0, *w)] = face_lo
        u1[(0, *w)] = (pr[(0, *w)] + flux) * keep_dn
        u1[(1, *w)] = ps[(1, *w)] - flux
        face_hi = COEF * (jnp.exp(thh[1, t]) + vv[(PLANES - 1, *w)])
        flux = face_hi * (uh[(1, *w)] - u0[(PLANES - 1, *w)])
        cx[(PLANES, *w)] = face_hi
        u1[(PLANES + 1, *w)] = (pr[(1, *w)] - flux) * keep_up
        u1[(PLANES, *w)] = ps[(0, *w)] + flux
    loop(0, 2, second)
    loop(PLANES - 2, PLANES, second)

    for copy in rings[0]:
        copy.wait_recv()
    for copy in rings[1]:
        copy.start()

    def probe(i, accs):
        new = []
        for b in range(2):
            cell = cells[b * BLK + i]
            row = u2[cell >> 7]
            one = jnp.sum(jnp.where(lane == (cell & (BLK - 1)), row, 0.0), axis=1, keepdims=True)
            new.append(jnp.where(lane == i, one, accs[b]))
        return tuple(new)

    zero = jnp.zeros((MEM, BLK), F32)
    pred = lax.fori_loop(0, BLK, probe, (zero, zero), unroll=16)
    for b in range(2):
        agb[g, y, :, tile(b)] = pred[b]

    def onward(i, yy):
        return [
            remote(agb.at[g, yy], agb.at[g, yy], ag2_s.at[d * NYR + i], ag2_r.at[d * NYR + i], s, ens_of(gg, y))
            for d, gg in enumerate(sub_g)
        ]

    order = [4, 3, 5, 2, 6, 1, 7]
    ag1 = {
        d: remote(agb.at[g, y], agb.at[g, y], ag1_s.at[d - 1], ag1_r.at[d - 1], s, ens_of(g, (y + d) % NYR))
        for d in order
    }
    for d in order:
        ag1[d].start()
    scaled = [
        (obs_ref[:, tile(b)] + noise_ref[:, tile(b)] - pred[b]) / var_ref[:, tile(b)] for b in range(2)
    ]
    for b in range(2):
        scw[g, :, tile(b)] = scaled[b]
    sc = [
        remote(scw.at[g], scw.at[g], sc_s.at[d], sc_r.at[d], s, ens_of(gg, y)) for d, gg in enumerate(sub_g)
    ]
    for copy in sc:
        copy.start()
    ag2 = onward(0, y)
    for copy in ag2:
        copy.start()

    def back(p):
        for t in range(LT):
            ost[t, pl.ds(p, MEM, PLANES), :] = u2[p * LT + t]

    loop(0, PLANES, back)
    for d in reversed(order):
        ag1[d].wait_recv()
        more = onward(d, (y + NYR - d) % NYR)
        for copy in more:
            copy.start()
        ag2 = ag2 + more
    for copy in rings[1]:
        copy.wait_recv()
    for copy in rings[2]:
        copy.start()
    for copy in sc:
        copy.wait_recv()

    own_class = agb[g].reshape(NYR * MEM, 2 * BLK)
    wide = scw[...].reshape(G * MEM, 2 * BLK)
    half_a = [dot(wide[:, tile(b)], own_class[:, tile(b)], NT) for b in range(2)]
    a_part[...] = jnp.concatenate(half_a, axis=1).reshape(G, MEM, BLK)
    a_win[1, g] = a_part[g]
    ax_up = [remote(a_part.at[gg], a_win.at[0, g], ax_s.at[gg], ax_r.at[g], s_up, ens_of(gg, y)) for gg in range(G)]
    ax_dn = [
        remote(a_part.at[gg], a_win.at[2, g], ax_s.at[G + gg], ax_r.at[G + g], s_dn, ens_of(gg, y)) for gg in range(G)
    ]
    ax_own = [
        remote(a_part.at[gg], a_win.at[1, g], ax_s.at[2 * G + d], ax_r.at[2 * G + d], s, ens_of(gg, y))
        for d, gg in enumerate(sub_g)
    ]

    @pl.when(has_up)
    def _():
        for copy in ax_up:
            copy.start()

    @pl.when(has_dn)
    def _():
        for copy in ax_dn:
            copy.start()

    for copy in ax_own:
        copy.start()
    for d, has in ((0, has_dn), (1, has_up)):

        @pl.when(jnp.logical_not(has))
        def _(d=d):
            a_win[2 * d] = jnp.zeros((G, MEM, BLK), F32)
            k_win[pl.ds(2 * d * G * 2, G * 2)] = jnp.zeros((G * 2, MEM, ALL), F32)

    for copy in ag2:
        copy.wait_recv()
    everyone = agb[...].reshape(ALL, 2 * BLK)
    anom[...] = everyone - jnp.sum(everyone, axis=0, keepdims=True) * (1.0 / ALL)
    for copy in rings[2]:
        copy.wait_recv()
    for copy in rings[3]:
        copy.start()
    for copy in ax_own:
        copy.wait_recv()
    for base, has in ((0, has_dn), (G, has_up)):

        @pl.when(has)
        def _(base=base):
            for gg in range(G):
                remote(a_part.at[0], a_win.at[0, g], ax_s.at[0], ax_r.at[base + gg], s, ens_of(gg, y)).wait_recv()

    for b in range(2):
        mixed = []
        for gg in range(G):
            mix = None
            for n in range(3):
                level = jnp.where(low, probe_taper[0, b, 2 * n].astype(F32), probe_taper[0, b, 2 * n + 1].astype(F32))
                term = a_win[n, gg] * level
                mix = term if mix is None else mix + term
            mixed.append(mix + pltpu.roll(mix, NZ, 1))
        mix = jnp.concatenate([jnp.where(low, mixed[q], mixed[q + 1]) for q in range(0, G, 2)], axis=1)
        corr = dot(mix * (1.0 / 256.0 / (ALL - 1)), anom[:, tile(b)], NN)
        gain = scaled[b] - corr / var_ref[:, tile(b)]
        gain_out[:, tile(b)] = gain
        kk = dot(gain, anom[:, tile(b)], NT)
        k_own[b] = kk
        k_win[(G + g) * 2 + b] = kk
    kx_up = [remote(k_own, k_win.at[pl.ds(g * 2, 2)], kx_s.at[gg], kx_r.at[g], s_up, ens_of(gg, y)) for gg in range(G)]
    kx_dn = [
        remote(k_own, k_win.at[pl.ds((2 * G + g) * 2, 2)], kx_s.at[G + gg], kx_r.at[G + g], s_dn, ens_of(gg, y))
        for gg in range(G)
    ]
    kx_own = [
        remote(k_own, k_win.at[pl.ds((G + g) * 2, 2)], kx_s.at[2 * G + d], kx_r.at[2 * G + d], s, ens_of(gg, y))
        for d, gg in enumerate(sub_g)
    ]

    @pl.when(has_up)
    def _():
        for copy in kx_up:
            copy.start()

    @pl.when(has_dn)
    def _():
        for copy in kx_dn:
            copy.start()

    for copy in kx_own:
        copy.start()
    for copy in rings[3]:
        copy.wait_recv()
    for copy in kx_own:
        copy.wait_recv()
    for base, has in ((0, has_dn), (G, has_up)):

        @pl.when(has)
        def _(base=base):
            for gg in range(G):
                remote(
                    k_own, k_win.at[pl.ds(g * 2, 2)], kx_s.at[0], kx_r.at[base + gg], s, ens_of(gg, y)
                ).wait_recv()

    for i in range(SPG):
        k = g * SPG + i
        j = pair_probes[0, k]
        at = (j >> 1) * (2 * G) + (j & 1)
        left_side = jnp.concatenate([k_win[at + 2 * gg] for gg in range(G)], axis=0)
        fields = jnp.concatenate([thg[yy, gg, i] for gg in range(G) for yy in range(NYR)], axis=0)
        us[:, i] = dot(left_side, fields, NN).reshape(G, MEM, BLK)
    for copy in sub_copies:
        copy.wait_send()
    ux = [
        remote(us.at[gg], upd_out.at[pl.ds(g * SPG, SPG)], ux_s.at[d], ux_r.at[d], s, ens_of(gg, y))
        for d, gg in enumerate(sub_g)
    ]
    for copy in ux:
        copy.start()
    for i in range(SPG):
        upd_out[g * SPG + i] = us[g, i]

    for d, p, dest, has in ends:

        @pl.when(has)
        def _(d=d):
            for copy in halo[d]:
                copy.wait_send()
            for copy in (ax_up, ax_dn)[d] + (kx_up, kx_dn)[d]:
                copy.wait_send()

    for copy in [q for each in rings for q in each] + list(ag1.values()) + ag2 + sc + ax_own + kx_own:
        copy.wait_send()
    for copy in ux:
        copy.wait()


def tail_kernel(
    cells_hbm, taper_hbm, pair_counts, prior_st, theta_st, upd, gain_in, prior_out, post_out, gain_out, post_st,
    pair_cells, pair_taper, sem_i, sem_p, sem_o,
):
    smalls = [
        pltpu.make_async_copy(a, b, sem_i.at[i])
        for i, (a, b) in enumerate(((cells_hbm, pair_cells), (taper_hbm, pair_taper)))
    ]
    for copy in smalls:
        copy.start()
    stores = [pltpu.make_async_copy(prior_st.at[t], prior_out.at[:, tile(t)], sem_p.at[t]) for t in range(LT)]
    for copy in stores:
        copy.start()
    gain_out[...] = gain_in[...]
    for copy in smalls:
        copy.wait()

    def add(k, carry):
        b = pair_cells[0, k]
        w = jnp.where(k < pair_counts[0], pair_taper[0, k].astype(F32) * (1.0 / 256.0), 0.0) * (1.0 / (ALL - 1))
        rows = pl.ds(b // LT, MEM, PLANES)
        post_st[b % LT, rows, :] = post_st[b % LT, rows, :] + w * upd[k]
        return carry

    lax.fori_loop(0, SLOTS, add, 0)
    late = [pltpu.make_async_copy(post_st.at[t], post_out.at[:, tile(t)], sem_o.at[t]) for t in range(LT)]
    for copy in late:
        copy.start()
    for copy in stores + late:
        copy.wait()


def shards(u, theta, observed, obs_noise, obs_var, probe_cells, pair_cells, pair_probes, pair_taper, pair_counts, probe_taper):
    shape = u.shape
    rows, cols = shape[0] * shape[1], shape[2]
    u, theta = u.reshape(rows, cols), theta.reshape(rows, cols)
    hbm = pl.BlockSpec(memory_space=pltpu.HBM)
    vmem = pl.BlockSpec(memory_space=pltpu.VMEM)
    big = (PLANES, MEM, cols)
    staged = (LT, rows, BLK)
    flat = (PLANES * LT, MEM, BLK)
    dma = pltpu.SemaphoreType.DMA

    def buf(*dims):
        return pltpu.VMEM(dims, F32)

    def stay(x):
        return pltpu.with_memory_space_constraint(x, pltpu.HBM)

    def ints(*dims):
        return pltpu.SMEM(dims, jnp.int32)

    def arr(*dims):
        return jax.ShapeDtypeStruct(dims, F32)

    prior_st, theta_st, gain, upd = pl.pallas_call(
        main_kernel,
        name="assimilate",
        out_shape=(arr(*staged), arr(*staged), arr(MEM, 2 * BLK), arr(SLOTS, MEM, BLK)),
        in_specs=[hbm] * 9,
        out_specs=(vmem,) * 4,
        scratch_shapes=[
            buf(*staged), buf(*big), buf(*flat), buf(*big),
            buf(PLANES + 1, MEM, cols), buf(*big), buf(*big), buf(*big),
            buf(2, MEM, cols), buf(2, LT, MEM, BLK), buf(2, MEM, cols), buf(2, MEM, cols),
            buf(PLANES + 2, MEM, cols), buf(*flat),
            buf(NYR, G, SPG, MEM, BLK), buf(G, NYR, MEM, 2 * BLK), buf(G, MEM, 2 * BLK), buf(ALL, 2 * BLK),
            buf(G, MEM, BLK), buf(3, G, MEM, BLK), buf(2, MEM, ALL), buf(3 * G * 2, MEM, ALL),
            buf(G, SPG, MEM, BLK), buf(SLOTS, MEM, BLK),
            buf(1, 2 * BLK), buf(MEM, 2 * BLK), buf(1, 2 * BLK),
            ints(2 * BLK), ints(1, SLOTS), ints(1, SLOTS), ints(1, 2, 6),
            dma((2 * LT,)), dma((7,)), dma((6,)), dma((6,)), dma((3,)), dma((3,)), dma((8,)), dma((8,)),
            dma((7,)), dma((7,)), dma((24,)), dma((24,)), dma((3,)), dma((3,)),
            dma((11,)), dma((11,)), dma((11,)), dma((11,)), dma((3,)), dma((3,)),
        ],
        compiler_params=pltpu.CompilerParams(
            collective_id=0, has_side_effects=True, vmem_limit_bytes=28 * 1024 * 1024
        ),
    )(
        *map(
            stay,
            (
                u, theta, observed.reshape(1, -1), obs_noise, obs_var.reshape(1, -1), probe_cells, pair_cells,
                pair_probes, probe_taper,
            ),
        )
    )
    prior, post, gain, _ = pl.pallas_call(
        tail_kernel,
        name="tail",
        out_shape=(arr(rows, cols), arr(rows, cols), arr(MEM, 2 * BLK), arr(*staged)),
        in_specs=[hbm, hbm, pl.BlockSpec(memory_space=pltpu.SMEM)] + [vmem] * 4,
        out_specs=(hbm, hbm, vmem, vmem),
        input_output_aliases={4: 3},
        scratch_shapes=[
            ints(1, SLOTS), ints(1, SLOTS), dma((2,)), dma((LT,)), dma((LT,)),
        ],
        compiler_params=pltpu.CompilerParams(vmem_limit_bytes=16 * 1024 * 1024),
    )(stay(pair_cells), stay(pair_taper), pair_counts, prior_st, theta_st, upd, gain)
    return prior.reshape(shape), post.reshape(shape), gain


def solution(mesh):
    return jax.shard_map(
        shards,
        mesh=mesh,
        in_specs=(
            P("ens", "space", None), P("ens", "space", None), P("space"), P("ens", "space"), P("space"), P("space"),
            P("space", None), P("space", None), P("space", None), P("space"), P("space", None, None),
        ),
        out_specs=(P("ens", "space", None), P("ens", "space", None), P("ens", "space")),
        check_vma=False,
    )
```

```python
import functools

import jax
import jax.numpy as jnp
from jax import lax
from jax.experimental import pallas as pl
from jax.experimental.pallas import tpu as pltpu
from jax.sharding import PartitionSpec as P

BLK = 128
NZ = 64
DT_STEP = 0.08
COEF = 0.5 * DT_STEP

NS = 16
NYR = 8
G = 4
PLANES = 16
LT = 16
MEM = 8
ALL = 256
SLOTS = 32
SPG = SLOTS // G

MESH = pl.DeviceIdType.MESH
HIGHEST = lax.Precision.HIGHEST
F32 = jnp.float32


def dot(a, b, dims):
    return lax.dot_general(a, b, (dims, ((), ())), precision=HIGHEST, preferred_element_type=F32)


NN = ((1,), (0,))
NT = ((1,), (1,))


def tile(t):
    return slice(t * BLK, (t + 1) * BLK)


def tiles(ref, *where):
    return [ref[(*where, slice(None), tile(t))] for t in range(LT)]


def put(ref, values, *where):
    for t in range(LT):
        ref[(*where, slice(None), tile(t))] = values[t]


def main_kernel(
    u_hbm, t_hbm, *refs
):
    smalls_hbm, refs = refs[:7], refs[7:]
    (
        ost, tst, gain_out, upd_out,
        ust, u0, th, vv, cx, cy, cz, cd, uh, thh, ps, pr, u1, u2,
        thg, agb, scw, anom, a_part, a_win, k_own, k_win, us, upd,
        obs_ref, noise_ref, var_ref, cells, pair_cells, pair_probes, probe_taper,
        in_sem, small_sem, halo_s, halo_r, sub_s, sub_r, ring_s, ring_r, ag1_s, ag1_r, ag2_s, ag2_r, sc_s, sc_r,
        ax_s, ax_r, kx_s, kx_r, ux_s, ux_r,
    ) = refs
    s = lax.axis_index("space")
    e = lax.axis_index("ens")
    xl, y, c = e // (2 * NYR), (e // 2) % NYR, e % 2
    g = xl * 2 + c
    has_up, has_dn = s < NS - 1, s > 0
    s_up, s_dn = jnp.minimum(s + 1, NS - 1), jnp.maximum(s - 1, 0)

    def ens_of(gg, yy):
        return (gg // 2) * (2 * NYR) + yy * 2 + gg % 2

    def remote(src, dst, ss, rs, space, ens):
        return pltpu.make_async_remote_copy(
            src_ref=src, dst_ref=dst, send_sem=ss, recv_sem=rs, device_id=(space, ens), device_id_type=MESH
        )

    sub_g = [(g + d) % G for d in range(1, G)]

    loads = []
    for k, (src, dst) in enumerate(((t_hbm, tst), (u_hbm, ust))):
        for t in range(LT):
            loads.append(pltpu.make_async_copy(src.at[:, tile(t)], dst.at[t], in_sem.at[k * LT + t]))
    for copy in loads:
        copy.start()
    smalls_vmem = (obs_ref, noise_ref, var_ref, cells, pair_cells, pair_probes, probe_taper)
    smalls = [pltpu.make_async_copy(a, b, small_sem.at[i]) for i, (a, b) in enumerate(zip(smalls_hbm, smalls_vmem))]
    for copy in smalls:
        copy.start()

    bar = pltpu.get_barrier_semaphore()
    for d in range(1, NYR):
        pl.semaphore_signal(bar, 1, device_id=(s, ens_of(g, (y + d) % NYR)), device_id_type=MESH)
    for gg in sub_g:
        pl.semaphore_signal(bar, 1, device_id=(s, ens_of(gg, y)), device_id_type=MESH)

    @pl.when(has_up)
    def _():
        for gg in range(G):
            pl.semaphore_signal(bar, 1, device_id=(s_up, ens_of(gg, y)), device_id_type=MESH)

    @pl.when(has_dn)
    def _():
        for gg in range(G):
            pl.semaphore_signal(bar, 1, device_id=(s_dn, ens_of(gg, y)), device_id_type=MESH)

    lane = lax.broadcasted_iota(jnp.int32, (MEM, BLK), 1)
    low = lane < NZ
    height = lane % NZ
    top = height == NZ - 1
    wall = (height == 0) | top

    def bring_theta(p):
        for t in range(LT):
            th[p * LT + t] = tst[t, pl.ds(p, MEM, PLANES), :]

    def bring_u(p):
        for t in range(LT):
            u0[p, :, tile(t)] = ust[t, pl.ds(p, MEM, PLANES), :]

    def viscosity(p):
        for t in range(LT):
            vv[p, :, tile(t)] = jnp.exp(th[p * LT + t])

    def loop(lo, hi, fn, unroll=2):
        def body(p, carry):
            fn(p)
            return carry

        lax.fori_loop(lo, hi, body, 0, unroll=unroll)

    def coefficients(p):
        def load(t):
            v = vv[p, :, tile(t % LT)]
            return v, pltpu.roll(v, NZ, 1)

        here = load(0)
        for t in range(LT):
            beside = load(t + 1)
            v = here[0]
            cy[p, :, tile(t)] = COEF * (v + jnp.where(low, here[1], beside[1]))
            cz[p, :, tile(t)] = jnp.where(top, 0.0, COEF * (v + pltpu.roll(v, BLK - 1, 1)))
            cd[p, :, tile(t)] = 1.0 - jnp.where(wall, COEF * (v + 1.0), 0.0)
            here = beside

    def face(p):
        for t in range(LT):
            cx[p, :, tile(t)] = COEF * (vv[p - 1, :, tile(t)] + vv[p, :, tile(t)])

    def step(src, off, p, lower, upper, emit):
        def load(t):
            v = src[p + off, :, tile(t % LT)]
            return v, pltpu.roll(v, NZ, 1)

        def flux_y(t, here, beside):
            f = cy[p, :, tile(t)] * (jnp.where(low, here[1], beside[1]) - here[0])
            return f, pltpu.roll(f, NZ, 1)

        here = first_one = load(0)
        before = last = load(LT - 1)
        f_prev = f_last = flux_y(LT - 1, last, first_one)
        for t in range(LT):
            beside = load(t + 1)
            f = flux_y(t, here, beside) if t < LT - 1 else f_last
            v = here[0]
            fz = cz[p, :, tile(t)] * (pltpu.roll(v, BLK - 1, 1) - v)
            new = cd[p, :, tile(t)] * v + ((f[0] - jnp.where(low, f_prev[1], f[1])) + (fz - pltpu.roll(fz, 1, 1)))
            if upper:
                new = new + cx[p + 1, :, tile(t)] * (src[p + 1 + off, :, tile(t)] - v)
            if lower:
                new = new - cx[p, :, tile(t)] * (v - src[p - 1 + off, :, tile(t)])
            emit(t, new)
            here, f_prev = beside, f

    def into(ref, *where):
        def emit(t, value):
            ref[(*where, slice(None), tile(t))] = value

        return emit

    for copy in loads[:LT] + smalls:
        copy.wait()
    loop(0, PLANES, bring_theta)

    def pick(k, carry):
        upd[k] = th[pair_cells[0, k]]
        return carry

    lax.fori_loop(0, SLOTS, pick, 0, unroll=4)
    thg[y, g] = upd[pl.ds(g * SPG, SPG)]
    sub_copies = [
        remote(upd.at[pl.ds(gg * SPG, SPG)], thg.at[y, g], sub_s.at[d], sub_r.at[d], s, ens_of(gg, y))
        for d, gg in enumerate(sub_g)
    ]

    rim = (0, 1, PLANES - 2, PLANES - 1)
    for p in rim:
        viscosity(p)
    for p in (0, PLANES - 1):
        coefficients(p)
    face(1)
    face(PLANES - 1)
    for copy in loads[LT:]:
        copy.wait()
    for p in rim:
        bring_u(p)
    step(u0, 0, PLANES - 1, True, False, into(ps, 0))
    step(u0, 0, 0, False, True, into(ps, 1))

    ends = ((0, PLANES - 1, s_up, has_up), (1, 0, s_dn, has_dn))
    halo = [
        [
            remote(th.at[pl.ds(p * LT, LT)], thh.at[d], halo_s.at[d * 3], halo_r.at[d * 3], dest, e),
            remote(u0.at[p], uh.at[d], halo_s.at[d * 3 + 1], halo_r.at[d * 3 + 1], dest, e),
            remote(ps.at[d], pr.at[d], halo_s.at[d * 3 + 2], halo_r.at[d * 3 + 2], dest, e),
        ]
        for d, p, dest, _ in ends
    ]
    pl.semaphore_wait(bar, NYR - 1 + G - 1 + G * has_up.astype(jnp.int32) + G * has_dn.astype(jnp.int32))
    for copy in sub_copies:
        copy.start()
    for d, p, dest, has in ends:

        @pl.when(has)
        def _(d=d):
            for copy in halo[d]:
                copy.start()

    right, left = ens_of(g, (y + 1) % NYR), ens_of(g, (y + NYR - 1) % NYR)
    half = G // 2

    def ring(n):
        a, b = (y + NYR - n) % NYR, (y + n) % NYR
        if n < 3:
            src_r, src_l = thg.at[a], thg.at[b]
        else:
            src_r, src_l = thg.at[a, pl.ds(0, half)], thg.at[b, pl.ds(half, half)]
        return [
            remote(src_r, src_r, ring_s.at[n * 2], ring_r.at[n * 2], s, right),
            remote(src_l, src_l, ring_s.at[n * 2 + 1], ring_r.at[n * 2 + 1], s, left),
        ]

    rings = [ring(n) for n in range(4)]

    loop(2, PLANES - 2, viscosity)
    loop(2, PLANES - 2, bring_u)
    loop(1, PLANES - 1, coefficients)
    loop(2, PLANES - 1, face, 1)

    def first(p):
        step(u0, 0, p, True, True, into(u1, p + 1))

    def second(p):
        def emit(t, value):
            u2[p * LT + t] = value

        step(u1, 1, p, True, True, emit)

    loop(1, PLANES - 1, first)
    for copy in sub_copies:
        copy.wait_recv()
    for copy in rings[0]:
        copy.start()
    loop(2, PLANES - 2, second)

    for copy in rings[0]:
        copy.wait_recv()
    for copy in rings[1]:
        copy.start()

    for d, p, dest, has in ends:

        @pl.when(jnp.logical_not((has_dn, has_up)[d]))
        def _(d=d):
            uh[d] = jnp.zeros_like(uh[d])
            thh[d] = jnp.zeros_like(thh[d])
            pr[d] = jnp.zeros_like(pr[d])

    for d, p, dest, has in ends:

        @pl.when((has_dn, has_up)[d])
        def _(d=d):
            for copy in halo[d]:
                copy.wait_recv()

    keep_dn = has_dn.astype(F32)
    keep_up = has_up.astype(F32)
    for t in range(LT):
        w = (slice(None), tile(t))
        face_lo = COEF * (jnp.exp(thh[0, t]) + vv[(0, *w)])
        flux = face_lo * (u0[(0, *w)] - uh[(0, *w)])
        cx[(0, *w)] = face_lo
        u1[(0, *w)] = (pr[(0, *w)] + flux) * keep_dn
        u1[(1, *w)] = ps[(1, *w)] - flux
        face_hi = COEF * (jnp.exp(thh[1, t]) + vv[(PLANES - 1, *w)])
        flux = face_hi * (uh[(1, *w)] - u0[(PLANES - 1, *w)])
        cx[(PLANES, *w)] = face_hi
        u1[(PLANES + 1, *w)] = (pr[(1, *w)] - flux) * keep_up
        u1[(PLANES, *w)] = ps[(0, *w)] + flux
    loop(0, 2, second)
    loop(PLANES - 2, PLANES, second)

    def probe(i, accs):
        new = []
        for b in range(2):
            cell = cells[b * BLK + i]
            row = u2[cell >> 7]
            one = jnp.sum(jnp.where(lane == (cell & (BLK - 1)), row, 0.0), axis=1, keepdims=True)
            new.append(jnp.where(lane == i, one, accs[b]))
        return tuple(new)

    zero = jnp.zeros((MEM, BLK), F32)
    pred = lax.fori_loop(0, BLK, probe, (zero, zero), unroll=16)
    for b in range(2):
        agb[g, y, :, tile(b)] = pred[b]

    def onward(i, yy):
        return [
            remote(agb.at[g, yy], agb.at[g, yy], ag2_s.at[d * NYR + i], ag2_r.at[d * NYR + i], s, ens_of(gg, y))
            for d, gg in enumerate(sub_g)
        ]

    order = [4, 3, 5, 2, 6, 1, 7]
    ag1 = {
        d: remote(agb.at[g, y], agb.at[g, y], ag1_s.at[d - 1], ag1_r.at[d - 1], s, ens_of(g, (y + d) % NYR))
        for d in order
    }
    for d in order:
        ag1[d].start()
    scaled = [
        (obs_ref[:, tile(b)] + noise_ref[:, tile(b)] - pred[b]) / var_ref[:, tile(b)] for b in range(2)
    ]
    for b in range(2):
        scw[g, :, tile(b)] = scaled[b]
    sc = [
        remote(scw.at[g], scw.at[g], sc_s.at[d], sc_r.at[d], s, ens_of(gg, y)) for d, gg in enumerate(sub_g)
    ]
    for copy in sc:
        copy.start()
    ag2 = onward(0, y)
    for copy in ag2:
        copy.start()

    def back(p):
        for t in range(LT):
            ost[t, pl.ds(p, MEM, PLANES), :] = u2[p * LT + t]

    loop(0, PLANES, back)
    for d in reversed(order):
        ag1[d].wait_recv()
        if d == 2:
            for copy in rings[1]:
                copy.wait_recv()
            for copy in rings[2]:
                copy.start()
        more = onward(d, (y + NYR - d) % NYR)
        for copy in more:
            copy.start()
        ag2 = ag2 + more
    for copy in sc:
        copy.wait_recv()

    own_class = agb[g].reshape(NYR * MEM, 2 * BLK)
    wide = scw[...].reshape(G * MEM, 2 * BLK)
    half_a = [dot(wide[:, tile(b)], own_class[:, tile(b)], NT) for b in range(2)]
    a_part[...] = jnp.concatenate(half_a, axis=1).reshape(G, MEM, BLK)
    a_win[1, g] = a_part[g]
    ax_up = [remote(a_part.at[gg], a_win.at[0, g], ax_s.at[gg], ax_r.at[g], s_up, ens_of(gg, y)) for gg in range(G)]
    ax_dn = [
        remote(a_part.at[gg], a_win.at[2, g], ax_s.at[G + gg], ax_r.at[G + g], s_dn, ens_of(gg, y)) for gg in range(G)
    ]
    ax_own = [
        remote(a_part.at[gg], a_win.at[1, g], ax_s.at[2 * G + d], ax_r.at[2 * G + d], s, ens_of(gg, y))
        for d, gg in enumerate(sub_g)
    ]

    @pl.when(has_up)
    def _():
        for copy in ax_up:
            copy.start()

    @pl.when(has_dn)
    def _():
        for copy in ax_dn:
            copy.start()

    for copy in ax_own:
        copy.start()
    for d, has in ((0, has_dn), (1, has_up)):

        @pl.when(jnp.logical_not(has))
        def _(d=d):
            a_win[2 * d] = jnp.zeros((G, MEM, BLK), F32)
            k_win[pl.ds(2 * d * G * 2, G * 2)] = jnp.zeros((G * 2, MEM, ALL), F32)

    for copy in ag2:
        copy.wait_recv()
    everyone = agb[...].reshape(ALL, 2 * BLK)
    anom[...] = everyone - jnp.sum(everyone, axis=0, keepdims=True) * (1.0 / ALL)
    for copy in ax_own:
        copy.wait_recv()
    for base, has in ((0, has_dn), (G, has_up)):

        @pl.when(has)
        def _(base=base):
            for gg in range(G):
                remote(a_part.at[0], a_win.at[0, g], ax_s.at[0], ax_r.at[base + gg], s, ens_of(gg, y)).wait_recv()

    for b in range(2):
        mixed = []
        for gg in range(G):
            mix = None
            for n in range(3):
                level = jnp.where(low, probe_taper[0, b, 2 * n].astype(F32), probe_taper[0, b, 2 * n + 1].astype(F32))
                term = a_win[n, gg] * level
                mix = term if mix is None else mix + term
            mixed.append(mix + pltpu.roll(mix, NZ, 1))
        mix = jnp.concatenate([jnp.where(low, mixed[q], mixed[q + 1]) for q in range(0, G, 2)], axis=1)
        corr = dot(mix * (1.0 / 256.0 / (ALL - 1)), anom[:, tile(b)], NN)
        gain = scaled[b] - corr / var_ref[:, tile(b)]
        gain_out[:, tile(b)] = gain
        kk = dot(gain, anom[:, tile(b)], NT)
        k_own[b] = kk
        k_win[(G + g) * 2 + b] = kk
    kx_up = [remote(k_own, k_win.at[pl.ds(g * 2, 2)], kx_s.at[gg], kx_r.at[g], s_up, ens_of(gg, y)) for gg in range(G)]
    kx_dn = [
        remote(k_own, k_win.at[pl.ds((2 * G + g) * 2, 2)], kx_s.at[G + gg], kx_r.at[G + g], s_dn, ens_of(gg, y))
        for gg in range(G)
    ]
    kx_own = [
        remote(k_own, k_win.at[pl.ds((G + g) * 2, 2)], kx_s.at[2 * G + d], kx_r.at[2 * G + d], s, ens_of(gg, y))
        for d, gg in enumerate(sub_g)
    ]

    @pl.when(has_up)
    def _():
        for copy in kx_up:
            copy.start()

    @pl.when(has_dn)
    def _():
        for copy in kx_dn:
            copy.start()

    for copy in kx_own:
        copy.start()
    for copy in rings[2]:
        copy.wait_recv()
    for copy in rings[3]:
        copy.start()
    for copy in rings[3]:
        copy.wait_recv()
    for copy in kx_own:
        copy.wait_recv()
    for base, has in ((0, has_dn), (G, has_up)):

        @pl.when(has)
        def _(base=base):
            for gg in range(G):
                remote(
                    k_own, k_win.at[pl.ds(g * 2, 2)], kx_s.at[0], kx_r.at[base + gg], s, ens_of(gg, y)
                ).wait_recv()

    for i in range(SPG):
        k = g * SPG + i
        j = pair_probes[0, k]
        at = (j >> 1) * (2 * G) + (j & 1)
        left_side = jnp.concatenate([k_win[at + 2 * gg] for gg in range(G)], axis=0)
        fields = jnp.concatenate([thg[yy, gg, i] for gg in range(G) for yy in range(NYR)], axis=0)
        us[:, i] = dot(left_side, fields, NN).reshape(G, MEM, BLK)
    for copy in sub_copies:
        copy.wait_send()
    ux = [
        remote(us.at[gg], upd_out.at[pl.ds(g * SPG, SPG)], ux_s.at[d], ux_r.at[d], s, ens_of(gg, y))
        for d, gg in enumerate(sub_g)
    ]
    for copy in ux:
        copy.start()
    for i in range(SPG):
        upd_out[g * SPG + i] = us[g, i]

    for d, p, dest, has in ends:

        @pl.when(has)
        def _(d=d):
            for copy in halo[d]:
                copy.wait_send()
            for copy in (ax_up, ax_dn)[d] + (kx_up, kx_dn)[d]:
                copy.wait_send()

    for copy in [q for each in rings for q in each] + list(ag1.values()) + ag2 + sc + ax_own + kx_own:
        copy.wait_send()
    for copy in ux:
        copy.wait()


def tail_kernel(
    cells_hbm, taper_hbm, pair_counts, prior_st, theta_st, upd, gain_in, prior_out, post_out, gain_out, post_st,
    pair_cells, pair_taper, sem_i, sem_p, sem_o,
):
    smalls = [
        pltpu.make_async_copy(a, b, sem_i.at[i])
        for i, (a, b) in enumerate(((cells_hbm, pair_cells), (taper_hbm, pair_taper)))
    ]
    for copy in smalls:
        copy.start()
    stores = [pltpu.make_async_copy(prior_st.at[t], prior_out.at[:, tile(t)], sem_p.at[t]) for t in range(LT)]
    for copy in stores:
        copy.start()
    gain_out[...] = gain_in[...]
    for copy in smalls:
        copy.wait()

    def add(k, carry):
        b = pair_cells[0, k]
        w = jnp.where(k < pair_counts[0], pair_taper[0, k].astype(F32) * (1.0 / 256.0), 0.0) * (1.0 / (ALL - 1))
        rows = pl.ds(b // LT, MEM, PLANES)
        post_st[b % LT, rows, :] = post_st[b % LT, rows, :] + w * upd[k]
        return carry

    lax.fori_loop(0, SLOTS, add, 0, unroll=8)
    late = [pltpu.make_async_copy(post_st.at[t], post_out.at[:, tile(t)], sem_o.at[t]) for t in range(LT)]
    for copy in late:
        copy.start()
    for copy in stores + late:
        copy.wait()


def shards(u, theta, observed, obs_noise, obs_var, probe_cells, pair_cells, pair_probes, pair_taper, pair_counts, probe_taper):
    shape = u.shape
    rows, cols = shape[0] * shape[1], shape[2]
    u, theta = u.reshape(rows, cols), theta.reshape(rows, cols)
    hbm = pl.BlockSpec(memory_space=pltpu.HBM)
    vmem = pl.BlockSpec(memory_space=pltpu.VMEM)
    big = (PLANES, MEM, cols)
    staged = (LT, rows, BLK)
    flat = (PLANES * LT, MEM, BLK)
    dma = pltpu.SemaphoreType.DMA

    def buf(*dims):
        return pltpu.VMEM(dims, F32)

    def stay(x):
        return pltpu.with_memory_space_constraint(x, pltpu.HBM)

    def ints(*dims):
        return pltpu.SMEM(dims, jnp.int32)

    def arr(*dims):
        return jax.ShapeDtypeStruct(dims, F32)

    prior_st, theta_st, gain, upd = pl.pallas_call(
        main_kernel,
        name="assimilate",
        out_shape=(arr(*staged), arr(*staged), arr(MEM, 2 * BLK), arr(SLOTS, MEM, BLK)),
        in_specs=[hbm] * 9,
        out_specs=(vmem,) * 4,
        scratch_shapes=[
            buf(*staged), buf(*big), buf(*flat), buf(*big),
            buf(PLANES + 1, MEM, cols), buf(*big), buf(*big), buf(*big),
            buf(2, MEM, cols), buf(2, LT, MEM, BLK), buf(2, MEM, cols), buf(2, MEM, cols),
            buf(PLANES + 2, MEM, cols), buf(*flat),
            buf(NYR, G, SPG, MEM, BLK), buf(G, NYR, MEM, 2 * BLK), buf(G, MEM, 2 * BLK), buf(ALL, 2 * BLK),
            buf(G, MEM, BLK), buf(3, G, MEM, BLK), buf(2, MEM, ALL), buf(3 * G * 2, MEM, ALL),
            buf(G, SPG, MEM, BLK), buf(SLOTS, MEM, BLK),
            buf(1, 2 * BLK), buf(MEM, 2 * BLK), buf(1, 2 * BLK),
            ints(2 * BLK), ints(1, SLOTS), ints(1, SLOTS), ints(1, 2, 6),
            dma((2 * LT,)), dma((7,)), dma((6,)), dma((6,)), dma((3,)), dma((3,)), dma((8,)), dma((8,)),
            dma((7,)), dma((7,)), dma((24,)), dma((24,)), dma((3,)), dma((3,)),
            dma((11,)), dma((11,)), dma((11,)), dma((11,)), dma((3,)), dma((3,)),
        ],
        compiler_params=pltpu.CompilerParams(
            collective_id=0, has_side_effects=True, vmem_limit_bytes=28 * 1024 * 1024
        ),
    )(
        *map(
            stay,
            (
                u, theta, observed.reshape(1, -1), obs_noise, obs_var.reshape(1, -1), probe_cells, pair_cells,
                pair_probes, probe_taper,
            ),
        )
    )
    prior, post, gain, _ = pl.pallas_call(
        tail_kernel,
        name="tail",
        out_shape=(arr(rows, cols), arr(rows, cols), arr(MEM, 2 * BLK), arr(*staged)),
        in_specs=[hbm, hbm, pl.BlockSpec(memory_space=pltpu.SMEM)] + [vmem] * 4,
        out_specs=(hbm, hbm, vmem, vmem),
        input_output_aliases={4: 3},
        scratch_shapes=[
            ints(1, SLOTS), ints(1, SLOTS), dma((2,)), dma((LT,)), dma((LT,)),
        ],
        compiler_params=pltpu.CompilerParams(vmem_limit_bytes=16 * 1024 * 1024),
    )(stay(pair_cells), stay(pair_taper), pair_counts, prior_st, theta_st, upd, gain)
    return prior.reshape(shape), post.reshape(shape), gain


def solution(mesh):
    return jax.shard_map(
        shards,
        mesh=mesh,
        in_specs=(
            P("ens", "space", None), P("ens", "space", None), P("space"), P("ens", "space"), P("space"), P("space"),
            P("space", None), P("space", None), P("space", None), P("space"), P("space", None, None),
        ),
        out_specs=(P("ens", "space", None), P("ens", "space", None), P("ens", "space")),
        check_vma=False,
    )
```

```python
import functools

import jax
import jax.numpy as jnp
from jax import lax
from jax.experimental import pallas as pl
from jax.experimental.pallas import tpu as pltpu
from jax.sharding import PartitionSpec as P

BLK = 128
NZ = 64
DT_STEP = 0.08
COEF = 0.5 * DT_STEP

NS = 16
NYR = 8
G = 4
PLANES = 16
LT = 16
MEM = 8
ALL = 256
SLOTS = 32
SPG = SLOTS // G

MESH = pl.DeviceIdType.MESH
HIGHEST = lax.Precision.HIGHEST
F32 = jnp.float32


def dot(a, b, dims):
    return lax.dot_general(a, b, (dims, ((), ())), precision=HIGHEST, preferred_element_type=F32)


NN = ((1,), (0,))
NT = ((1,), (1,))


def tile(t):
    return slice(t * BLK, (t + 1) * BLK)


def tiles(ref, *where):
    return [ref[(*where, slice(None), tile(t))] for t in range(LT)]


def put(ref, values, *where):
    for t in range(LT):
        ref[(*where, slice(None), tile(t))] = values[t]


def main_kernel(
    u_hbm, t_hbm, *refs
):
    smalls_hbm, refs = refs[:7], refs[7:]
    (
        ost, tst, gain_out, upd_out,
        ust, u0, th, vv, cx, cy, cz, cd, uh, thh, ps, pr, u1, u2,
        thg, agb, scw, anom, a_part, a_win, k_own, k_win, us, upd,
        obs_ref, noise_ref, var_ref, cells, pair_cells, pair_probes, probe_taper,
        in_sem, small_sem, halo_s, halo_r, sub_s, sub_r, ring_s, ring_r, ag1_s, ag1_r, ag2_s, ag2_r, sc_s, sc_r,
        ax_s, ax_r, kx_s, kx_r, ux_s, ux_r,
    ) = refs
    s = lax.axis_index("space")
    e = lax.axis_index("ens")
    xl, y, c = e // (2 * NYR), (e // 2) % NYR, e % 2
    g = xl * 2 + c
    has_up, has_dn = s < NS - 1, s > 0
    s_up, s_dn = jnp.minimum(s + 1, NS - 1), jnp.maximum(s - 1, 0)

    def ens_of(gg, yy):
        return (gg // 2) * (2 * NYR) + yy * 2 + gg % 2

    def remote(src, dst, ss, rs, space, ens):
        return pltpu.make_async_remote_copy(
            src_ref=src, dst_ref=dst, send_sem=ss, recv_sem=rs, device_id=(space, ens), device_id_type=MESH
        )

    sub_g = [(g + d) % G for d in range(1, G)]

    bar = pltpu.get_barrier_semaphore()
    for d in range(1, NYR):
        pl.semaphore_signal(bar, 1, device_id=(s, ens_of(g, (y + d) % NYR)), device_id_type=MESH)
    for gg in sub_g:
        pl.semaphore_signal(bar, 1, device_id=(s, ens_of(gg, y)), device_id_type=MESH)

    @pl.when(has_up)
    def _():
        for gg in range(G):
            pl.semaphore_signal(bar, 1, device_id=(s_up, ens_of(gg, y)), device_id_type=MESH)

    @pl.when(has_dn)
    def _():
        for gg in range(G):
            pl.semaphore_signal(bar, 1, device_id=(s_dn, ens_of(gg, y)), device_id_type=MESH)

    loads = []
    for k, (src, dst) in enumerate(((t_hbm, tst), (u_hbm, ust))):
        for t in range(LT):
            loads.append(pltpu.make_async_copy(src.at[:, tile(t)], dst.at[t], in_sem.at[k * LT + t]))
    for copy in loads:
        copy.start()
    smalls_vmem = (obs_ref, noise_ref, var_ref, cells, pair_cells, pair_probes, probe_taper)
    smalls = [pltpu.make_async_copy(a, b, small_sem.at[i]) for i, (a, b) in enumerate(zip(smalls_hbm, smalls_vmem))]
    for copy in smalls:
        copy.start()

    lane = lax.broadcasted_iota(jnp.int32, (MEM, BLK), 1)
    low = lane < NZ
    height = lane % NZ
    top = height == NZ - 1
    wall = (height == 0) | top

    def bring_theta(p):
        for t in range(LT):
            th[p * LT + t] = tst[t, pl.ds(p, MEM, PLANES), :]

    def bring_u(p):
        for t in range(LT):
            u0[p, :, tile(t)] = ust[t, pl.ds(p, MEM, PLANES), :]

    def viscosity(p):
        for t in range(LT):
            vv[p, :, tile(t)] = jnp.exp(th[p * LT + t])

    def loop(lo, hi, fn, unroll=2):
        def body(p, carry):
            fn(p)
            return carry

        lax.fori_loop(lo, hi, body, 0, unroll=unroll)

    def coefficients(p):
        def load(t):
            v = vv[p, :, tile(t % LT)]
            return v, pltpu.roll(v, NZ, 1)

        here = load(0)
        for t in range(LT):
            beside = load(t + 1)
            v = here[0]
            cy[p, :, tile(t)] = COEF * (v + jnp.where(low, here[1], beside[1]))
            cz[p, :, tile(t)] = jnp.where(top, 0.0, COEF * (v + pltpu.roll(v, BLK - 1, 1)))
            cd[p, :, tile(t)] = 1.0 - jnp.where(wall, COEF * (v + 1.0), 0.0)
            here = beside

    def face(p):
        for t in range(LT):
            cx[p, :, tile(t)] = COEF * (vv[p - 1, :, tile(t)] + vv[p, :, tile(t)])

    def step(src, off, p, lower, upper, emit):
        def load(t):
            v = src[p + off, :, tile(t % LT)]
            return v, pltpu.roll(v, NZ, 1)

        def flux_y(t, here, beside):
            f = cy[p, :, tile(t)] * (jnp.where(low, here[1], beside[1]) - here[0])
            return f, pltpu.roll(f, NZ, 1)

        here = first_one = load(0)
        before = last = load(LT - 1)
        f_prev = f_last = flux_y(LT - 1, last, first_one)
        for t in range(LT):
            beside = load(t + 1)
            f = flux_y(t, here, beside) if t < LT - 1 else f_last
            v = here[0]
            fz = cz[p, :, tile(t)] * (pltpu.roll(v, BLK - 1, 1) - v)
            new = cd[p, :, tile(t)] * v + ((f[0] - jnp.where(low, f_prev[1], f[1])) + (fz - pltpu.roll(fz, 1, 1)))
            if upper:
                new = new + cx[p + 1, :, tile(t)] * (src[p + 1 + off, :, tile(t)] - v)
            if lower:
                new = new - cx[p, :, tile(t)] * (v - src[p - 1 + off, :, tile(t)])
            emit(t, new)
            here, f_prev = beside, f

    def into(ref, *where):
        def emit(t, value):
            ref[(*where, slice(None), tile(t))] = value

        return emit

    for copy in loads[:LT] + smalls:
        copy.wait()
    loop(0, PLANES, bring_theta)

    def pick(k, carry):
        upd[k] = th[pair_cells[0, k]]
        return carry

    lax.fori_loop(0, SLOTS, pick, 0, unroll=4)
    thg[y, g] = upd[pl.ds(g * SPG, SPG)]
    sub_copies = [
        remote(upd.at[pl.ds(gg * SPG, SPG)], thg.at[y, g], sub_s.at[d], sub_r.at[d], s, ens_of(gg, y))
        for d, gg in enumerate(sub_g)
    ]

    rim = (0, 1, PLANES - 2, PLANES - 1)
    for p in rim:
        viscosity(p)
    for p in (0, PLANES - 1):
        coefficients(p)
    face(1)
    face(PLANES - 1)
    for copy in loads[LT:]:
        copy.wait()
    for p in rim:
        bring_u(p)
    step(u0, 0, PLANES - 1, True, False, into(ps, 0))
    step(u0, 0, 0, False, True, into(ps, 1))

    ends = ((0, PLANES - 1, s_up, has_up), (1, 0, s_dn, has_dn))
    halo = [
        [
            remote(th.at[pl.ds(p * LT, LT)], thh.at[d], halo_s.at[d * 3], halo_r.at[d * 3], dest, e),
            remote(u0.at[p], uh.at[d], halo_s.at[d * 3 + 1], halo_r.at[d * 3 + 1], dest, e),
            remote(ps.at[d], pr.at[d], halo_s.at[d * 3 + 2], halo_r.at[d * 3 + 2], dest, e),
        ]
        for d, p, dest, _ in ends
    ]
    pl.semaphore_wait(bar, NYR - 1 + G - 1 + G * has_up.astype(jnp.int32) + G * has_dn.astype(jnp.int32))
    for copy in sub_copies:
        copy.start()
    for d, p, dest, has in ends:

        @pl.when(has)
        def _(d=d):
            for copy in halo[d]:
                copy.start()

    right, left = ens_of(g, (y + 1) % NYR), ens_of(g, (y + NYR - 1) % NYR)
    half = G // 2

    def ring(n):
        a, b = (y + NYR - n) % NYR, (y + n) % NYR
        if n < 3:
            src_r, src_l = thg.at[a], thg.at[b]
        else:
            src_r, src_l = thg.at[a, pl.ds(0, half)], thg.at[b, pl.ds(half, half)]
        return [
            remote(src_r, src_r, ring_s.at[n * 2], ring_r.at[n * 2], s, right),
            remote(src_l, src_l, ring_s.at[n * 2 + 1], ring_r.at[n * 2 + 1], s, left),
        ]

    rings = [ring(n) for n in range(4)]

    loop(2, PLANES - 2, viscosity)
    loop(2, PLANES - 2, bring_u)
    loop(1, PLANES - 1, coefficients)
    loop(2, PLANES - 1, face, 1)

    def first(p):
        step(u0, 0, p, True, True, into(u1, p + 1))

    def second(p):
        def emit(t, value):
            u2[p * LT + t] = value

        step(u1, 1, p, True, True, emit)

    loop(1, PLANES - 1, first)
    for copy in sub_copies:
        copy.wait_recv()
    for copy in rings[0]:
        copy.start()
    loop(2, PLANES - 2, second)

    for copy in rings[0]:
        copy.wait_recv()
    for copy in rings[1]:
        copy.start()

    for d, p, dest, has in ends:

        @pl.when(jnp.logical_not((has_dn, has_up)[d]))
        def _(d=d):
            uh[d] = jnp.zeros_like(uh[d])
            thh[d] = jnp.zeros_like(thh[d])
            pr[d] = jnp.zeros_like(pr[d])

    for d, p, dest, has in ends:

        @pl.when((has_dn, has_up)[d])
        def _(d=d):
            for copy in halo[d]:
                copy.wait_recv()

    keep_dn = has_dn.astype(F32)
    keep_up = has_up.astype(F32)
    for t in range(LT):
        w = (slice(None), tile(t))
        face_lo = COEF * (jnp.exp(thh[0, t]) + vv[(0, *w)])
        flux = face_lo * (u0[(0, *w)] - uh[(0, *w)])
        cx[(0, *w)] = face_lo
        u1[(0, *w)] = (pr[(0, *w)] + flux) * keep_dn
        u1[(1, *w)] = ps[(1, *w)] - flux
        face_hi = COEF * (jnp.exp(thh[1, t]) + vv[(PLANES - 1, *w)])
        flux = face_hi * (uh[(1, *w)] - u0[(PLANES - 1, *w)])
        cx[(PLANES, *w)] = face_hi
        u1[(PLANES + 1, *w)] = (pr[(1, *w)] - flux) * keep_up
        u1[(PLANES, *w)] = ps[(0, *w)] + flux
    loop(0, 2, second)
    loop(PLANES - 2, PLANES, second)

    def probe(i, accs):
        new = []
        for b in range(2):
            cell = cells[b * BLK + i]
            row = u2[cell >> 7]
            one = jnp.sum(jnp.where(lane == (cell & (BLK - 1)), row, 0.0), axis=1, keepdims=True)
            new.append(jnp.where(lane == i, one, accs[b]))
        return tuple(new)

    zero = jnp.zeros((MEM, BLK), F32)
    pred = lax.fori_loop(0, BLK, probe, (zero, zero), unroll=16)
    for b in range(2):
        agb[g, y, :, tile(b)] = pred[b]

    def onward(i, yy):
        return [
            remote(agb.at[g, yy], agb.at[g, yy], ag2_s.at[d * NYR + i], ag2_r.at[d * NYR + i], s, ens_of(gg, y))
            for d, gg in enumerate(sub_g)
        ]

    order = [4, 3, 5, 2, 6, 1, 7]
    ag1 = {
        d: remote(agb.at[g, y], agb.at[g, y], ag1_s.at[d - 1], ag1_r.at[d - 1], s, ens_of(g, (y + d) % NYR))
        for d in order
    }
    for d in order:
        ag1[d].start()
    scaled = [
        (obs_ref[:, tile(b)] + noise_ref[:, tile(b)] - pred[b]) / var_ref[:, tile(b)] for b in range(2)
    ]
    for b in range(2):
        scw[g, :, tile(b)] = scaled[b]
    sc = [
        remote(scw.at[g], scw.at[g], sc_s.at[d], sc_r.at[d], s, ens_of(gg, y)) for d, gg in enumerate(sub_g)
    ]
    for copy in sc:
        copy.start()
    ag2 = onward(0, y)
    for copy in ag2:
        copy.start()

    def back(p):
        for t in range(LT):
            ost[t, pl.ds(p, MEM, PLANES), :] = u2[p * LT + t]

    loop(0, PLANES, back)
    for d in reversed(order):
        ag1[d].wait_recv()
        if d == 2:
            for copy in rings[1]:
                copy.wait_recv()
            for copy in rings[2]:
                copy.start()
        more = onward(d, (y + NYR - d) % NYR)
        for copy in more:
            copy.start()
        ag2 = ag2 + more
    for copy in sc:
        copy.wait_recv()

    own_class = agb[g].reshape(NYR * MEM, 2 * BLK)
    wide = scw[...].reshape(G * MEM, 2 * BLK)
    half_a = [dot(wide[:, tile(b)], own_class[:, tile(b)], NT) for b in range(2)]
    a_part[...] = jnp.concatenate(half_a, axis=1).reshape(G, MEM, BLK)
    a_win[1, g] = a_part[g]
    ax_up = [remote(a_part.at[gg], a_win.at[0, g], ax_s.at[gg], ax_r.at[g], s_up, ens_of(gg, y)) for gg in range(G)]
    ax_dn = [
        remote(a_part.at[gg], a_win.at[2, g], ax_s.at[G + gg], ax_r.at[G + g], s_dn, ens_of(gg, y)) for gg in range(G)
    ]
    ax_own = [
        remote(a_part.at[gg], a_win.at[1, g], ax_s.at[2 * G + d], ax_r.at[2 * G + d], s, ens_of(gg, y))
        for d, gg in enumerate(sub_g)
    ]

    @pl.when(has_up)
    def _():
        for copy in ax_up:
            copy.start()

    @pl.when(has_dn)
    def _():
        for copy in ax_dn:
            copy.start()

    for copy in ax_own:
        copy.start()
    for d, has in ((0, has_dn), (1, has_up)):

        @pl.when(jnp.logical_not(has))
        def _(d=d):
            a_win[2 * d] = jnp.zeros((G, MEM, BLK), F32)
            k_win[pl.ds(2 * d * G * 2, G * 2)] = jnp.zeros((G * 2, MEM, ALL), F32)

    for copy in ag2:
        copy.wait_recv()
    everyone = agb[...].reshape(ALL, 2 * BLK)
    anom[...] = everyone - jnp.sum(everyone, axis=0, keepdims=True) * (1.0 / ALL)
    for copy in ax_own:
        copy.wait_recv()
    for base, has in ((0, has_dn), (G, has_up)):

        @pl.when(has)
        def _(base=base):
            for gg in range(G):
                remote(a_part.at[0], a_win.at[0, g], ax_s.at[0], ax_r.at[base + gg], s, ens_of(gg, y)).wait_recv()

    for b in range(2):
        mixed = []
        for gg in range(G):
            mix = None
            for n in range(3):
                level = jnp.where(low, probe_taper[0, b, 2 * n].astype(F32), probe_taper[0, b, 2 * n + 1].astype(F32))
                term = a_win[n, gg] * level
                mix = term if mix is None else mix + term
            mixed.append(mix + pltpu.roll(mix, NZ, 1))
        mix = jnp.concatenate([jnp.where(low, mixed[q], mixed[q + 1]) for q in range(0, G, 2)], axis=1)
        corr = dot(mix * (1.0 / 256.0 / (ALL - 1)), anom[:, tile(b)], NN)
        gain = scaled[b] - corr / var_ref[:, tile(b)]
        gain_out[:, tile(b)] = gain
        kk = dot(gain, anom[:, tile(b)], NT)
        k_own[b] = kk
        k_win[(G + g) * 2 + b] = kk
    kx_up = [remote(k_own, k_win.at[pl.ds(g * 2, 2)], kx_s.at[gg], kx_r.at[g], s_up, ens_of(gg, y)) for gg in range(G)]
    kx_dn = [
        remote(k_own, k_win.at[pl.ds((2 * G + g) * 2, 2)], kx_s.at[G + gg], kx_r.at[G + g], s_dn, ens_of(gg, y))
        for gg in range(G)
    ]
    kx_own = [
        remote(k_own, k_win.at[pl.ds((G + g) * 2, 2)], kx_s.at[2 * G + d], kx_r.at[2 * G + d], s, ens_of(gg, y))
        for d, gg in enumerate(sub_g)
    ]

    @pl.when(has_up)
    def _():
        for copy in kx_up:
            copy.start()

    @pl.when(has_dn)
    def _():
        for copy in kx_dn:
            copy.start()

    for copy in kx_own:
        copy.start()
    for copy in rings[2]:
        copy.wait_recv()
    for copy in rings[3]:
        copy.start()
    for copy in rings[3]:
        copy.wait_recv()
    for copy in kx_own:
        copy.wait_recv()
    for base, has in ((0, has_dn), (G, has_up)):

        @pl.when(has)
        def _(base=base):
            for gg in range(G):
                remote(
                    k_own, k_win.at[pl.ds(g * 2, 2)], kx_s.at[0], kx_r.at[base + gg], s, ens_of(gg, y)
                ).wait_recv()

    for i in range(SPG):
        k = g * SPG + i
        j = pair_probes[0, k]
        at = (j >> 1) * (2 * G) + (j & 1)
        left_side = jnp.concatenate([k_win[at + 2 * gg] for gg in range(G)], axis=0)
        fields = jnp.concatenate([thg[yy, gg, i] for gg in range(G) for yy in range(NYR)], axis=0)
        us[:, i] = dot(left_side, fields, NN).reshape(G, MEM, BLK)
    for copy in sub_copies:
        copy.wait_send()
    ux = [
        remote(us.at[gg], upd_out.at[pl.ds(g * SPG, SPG)], ux_s.at[d], ux_r.at[d], s, ens_of(gg, y))
        for d, gg in enumerate(sub_g)
    ]
    for copy in ux:
        copy.start()
    for i in range(SPG):
        upd_out[g * SPG + i] = us[g, i]

    for d, p, dest, has in ends:

        @pl.when(has)
        def _(d=d):
            for copy in halo[d]:
                copy.wait_send()
            for copy in (ax_up, ax_dn)[d] + (kx_up, kx_dn)[d]:
                copy.wait_send()

    for copy in [q for each in rings for q in each] + list(ag1.values()) + ag2 + sc + ax_own + kx_own:
        copy.wait_send()
    for copy in ux:
        copy.wait()


def tail_kernel(
    cells_hbm, taper_hbm, pair_counts, prior_st, theta_st, upd, gain_in, prior_out, post_out, gain_out, post_st,
    pair_cells, pair_taper, sem_i, sem_p, sem_o,
):
    smalls = [
        pltpu.make_async_copy(a, b, sem_i.at[i])
        for i, (a, b) in enumerate(((cells_hbm, pair_cells), (taper_hbm, pair_taper)))
    ]
    for copy in smalls:
        copy.start()
    stores = [pltpu.make_async_copy(prior_st.at[t], prior_out.at[:, tile(t)], sem_p.at[t]) for t in range(LT)]
    for copy in stores:
        copy.start()
    gain_out[...] = gain_in[...]
    for copy in smalls:
        copy.wait()

    def add(k, carry):
        b = pair_cells[0, k]
        w = jnp.where(k < pair_counts[0], pair_taper[0, k].astype(F32) * (1.0 / 256.0), 0.0) * (1.0 / (ALL - 1))
        rows = pl.ds(b // LT, MEM, PLANES)
        post_st[b % LT, rows, :] = post_st[b % LT, rows, :] + w * upd[k]
        return carry

    lax.fori_loop(0, SLOTS, add, 0, unroll=8)
    late = [pltpu.make_async_copy(post_st.at[t], post_out.at[:, tile(t)], sem_o.at[t]) for t in range(LT)]
    for copy in late:
        copy.start()
    for copy in stores + late:
        copy.wait()


def shards(u, theta, observed, obs_noise, obs_var, probe_cells, pair_cells, pair_probes, pair_taper, pair_counts, probe_taper):
    shape = u.shape
    rows, cols = shape[0] * shape[1], shape[2]
    u, theta = u.reshape(rows, cols), theta.reshape(rows, cols)
    hbm = pl.BlockSpec(memory_space=pltpu.HBM)
    vmem = pl.BlockSpec(memory_space=pltpu.VMEM)
    big = (PLANES, MEM, cols)
    staged = (LT, rows, BLK)
    flat = (PLANES * LT, MEM, BLK)
    dma = pltpu.SemaphoreType.DMA

    def buf(*dims):
        return pltpu.VMEM(dims, F32)

    def stay(x):
        return pltpu.with_memory_space_constraint(x, pltpu.HBM)

    def ints(*dims):
        return pltpu.SMEM(dims, jnp.int32)

    def arr(*dims):
        return jax.ShapeDtypeStruct(dims, F32)

    prior_st, theta_st, gain, upd = pl.pallas_call(
        main_kernel,
        name="assimilate",
        out_shape=(arr(*staged), arr(*staged), arr(MEM, 2 * BLK), arr(SLOTS, MEM, BLK)),
        in_specs=[hbm] * 9,
        out_specs=(vmem,) * 4,
        scratch_shapes=[
            buf(*staged), buf(*big), buf(*flat), buf(*big),
            buf(PLANES + 1, MEM, cols), buf(*big), buf(*big), buf(*big),
            buf(2, MEM, cols), buf(2, LT, MEM, BLK), buf(2, MEM, cols), buf(2, MEM, cols),
            buf(PLANES + 2, MEM, cols), buf(*flat),
            buf(NYR, G, SPG, MEM, BLK), buf(G, NYR, MEM, 2 * BLK), buf(G, MEM, 2 * BLK), buf(ALL, 2 * BLK),
            buf(G, MEM, BLK), buf(3, G, MEM, BLK), buf(2, MEM, ALL), buf(3 * G * 2, MEM, ALL),
            buf(G, SPG, MEM, BLK), buf(SLOTS, MEM, BLK),
            buf(1, 2 * BLK), buf(MEM, 2 * BLK), buf(1, 2 * BLK),
            ints(2 * BLK), ints(1, SLOTS), ints(1, SLOTS), ints(1, 2, 6),
            dma((2 * LT,)), dma((7,)), dma((6,)), dma((6,)), dma((3,)), dma((3,)), dma((8,)), dma((8,)),
            dma((7,)), dma((7,)), dma((24,)), dma((24,)), dma((3,)), dma((3,)),
            dma((11,)), dma((11,)), dma((11,)), dma((11,)), dma((3,)), dma((3,)),
        ],
        compiler_params=pltpu.CompilerParams(
            collective_id=0, has_side_effects=True, vmem_limit_bytes=28 * 1024 * 1024
        ),
    )(
        *map(
            stay,
            (
                u, theta, observed.reshape(1, -1), obs_noise, obs_var.reshape(1, -1), probe_cells, pair_cells,
                pair_probes, probe_taper,
            ),
        )
    )
    prior, post, gain, _ = pl.pallas_call(
        tail_kernel,
        name="tail",
        out_shape=(arr(rows, cols), arr(rows, cols), arr(MEM, 2 * BLK), arr(*staged)),
        in_specs=[hbm, hbm, pl.BlockSpec(memory_space=pltpu.SMEM)] + [vmem] * 4,
        out_specs=(hbm, hbm, vmem, vmem),
        input_output_aliases={4: 3},
        scratch_shapes=[
            ints(1, SLOTS), ints(1, SLOTS), dma((2,)), dma((LT,)), dma((LT,)),
        ],
        compiler_params=pltpu.CompilerParams(vmem_limit_bytes=16 * 1024 * 1024),
    )(stay(pair_cells), stay(pair_taper), pair_counts, prior_st, theta_st, upd, gain)
    return prior.reshape(shape), post.reshape(shape), gain


def solution(mesh):
    return jax.shard_map(
        shards,
        mesh=mesh,
        in_specs=(
            P("ens", "space", None), P("ens", "space", None), P("space"), P("ens", "space"), P("space"), P("space"),
            P("space", None), P("space", None), P("space", None), P("space"), P("space", None, None),
        ),
        out_specs=(P("ens", "space", None), P("ens", "space", None), P("ens", "space")),
        check_vma=False,
    )
```
